32 devices in a mesh: dom: 4 (over z), sub: 8 (over y, x, core).
Axes of the slice: x: 2, y: 2, z: 4, core: 2. Of those that a mesh axis runs over, the one named last changes fastest.
Arguments:
- state: float32 [9, 120, 512], P(None, None, ('dom', 'sub')), may hold values from -6 to 6
- ck_matrices: float32 [3, 120, 120], replicated, may hold values from -2 to 2
- vol_matrices: float32 [3, 120, 120], replicated, may hold values from -0.5 to 0.5
- face_project: float32 [4, 36, 120], replicated, may hold values from -0.5 to 0.5
- face_lift: float32 [4, 120, 36], replicated, may hold values from -1 to 1
- face_turn: float32 [3, 36, 36], replicated, may hold values from -1 to 1
- star_matrices: float32 [3, 9, 9, 512], P(None, None, None, ('dom', 'sub')), may hold values from -0.75 to 0.75
- flux_local: float32 [4, 9, 9, 512], P(None, None, None, ('dom', 'sub')), may hold values from -0.75 to 0.75
- flux_neighbor: float32 [4, 9, 9, 512], P(None, None, None, ('dom', 'sub')), may hold values from -0.75 to 0.75
- cluster: int32 [512], P(('dom', 'sub')), may hold values from 0 to 2
- send_elements: int32 [4, 8, 6, 4], P('dom', 'sub'), may hold values from 0 to 15, as said below
- send_faces: int32 [4, 8, 6, 4], P('dom', 'sub'), may hold values from 0 to 3
- neighbor_source: int32 [4, 512], P(None, ('dom', 'sub')), may hold values from 0 to 39, as said below
- neighbor_face: int32 [4, 512], P(None, ('dom', 'sub')), may hold values from 0 to 3, as said below
- neighbor_turn: int32 [4, 512], P(None, ('dom', 'sub')), may hold values from 0 to 2
Outputs:
- state_out: float32 [9, 120, 512], P(None, None, ('dom', 'sub'))
The draws below stay inside these ranges and needn't reach their ends.
Inputs may be any that keep to these rules, and one draw needn't show every extreme that they name: `send_elements`: slot indices of a partition; every entry sends an existing element. `neighbor_source`: values of 16 or more name received slots; every partition uses every one of its received slots exactly once, except slots from beyond the ends of the chain, which are never used. `neighbor_face`: read only where the neighbour is a local element.
All inputs are finite; a program needn't handle non-finite values.
Results may differ from the reference program's by a relative error of at most 0.0001.
Values sent between devices are 32-bit elements; how exact they have to be, the bound alone decides.
A program may use at most 64 MiB of HBM per device.

```python
import jax
import jax.numpy as jnp
from jax import lax

NB = 120
NQ = 9
NFB = 36
ORDER = 8
SUBSTEPS = 4
E_DEV = 16
SLOT = 4
ELEMENTS = 512
N_DOM = 4
N_SUB = 8


def graph_parts(key):
    base = jax.random.fold_in(key, 7)
    keys = jax.random.split(base, 5)
    shape = (N_DOM, N_SUB, 6, SLOT)
    send_elements = jax.random.randint(keys[0], shape, 0, E_DEV, dtype=jnp.int32)
    send_faces = jax.random.randint(keys[1], shape, 0, 4, dtype=jnp.int32)
    devcount = N_DOM * N_SUB
    incoming = 6 * SLOT
    orders = jax.vmap(lambda single: jax.random.permutation(single, 4 * E_DEV))(jax.random.split(keys[2], devcount))
    ranks = jnp.argsort(orders, axis=1).astype(jnp.int32)
    directions = ((0, 1), (0, -1), (1, 1), (1, -1), (1, 2), (1, -2))
    faces_in = []
    usable = []
    dom_index = jnp.arange(N_DOM, dtype=jnp.int32)[:, None] + jnp.zeros((N_DOM, N_SUB), jnp.int32)
    for place in range(6):
        axis_number, offset = directions[place]
        faces_in.append(jnp.roll(send_faces[:, :, place, :], offset, axis=axis_number))
        if place == 0:
            flag = dom_index >= 1
        elif place == 1:
            flag = dom_index <= N_DOM - 2
        else:
            flag = dom_index >= 0
        usable.append(jnp.broadcast_to(flag[:, :, None], (N_DOM, N_SUB, SLOT)))
    slot_face = jnp.stack(faces_in, axis=2).reshape(devcount, incoming)
    slot_usable = jnp.stack(usable, axis=2).reshape(devcount, incoming)
    clipped = jnp.minimum(ranks, incoming - 1)
    remote = (ranks < incoming) & jnp.take_along_axis(slot_usable, clipped, axis=1)
    remote_face = jnp.take_along_axis(slot_face, clipped, axis=1)
    local_source = jax.random.randint(keys[3], (devcount, 4 * E_DEV), 0, E_DEV, dtype=jnp.int32)
    local_face = jax.random.randint(keys[4], (devcount, 4 * E_DEV), 0, 4, dtype=jnp.int32)
    source = jnp.where(remote, E_DEV + ranks, local_source)
    face = jnp.where(remote, remote_face, local_face)
    source = source.reshape(devcount, 4, E_DEV).transpose(1, 0, 2).reshape(4, devcount * E_DEV)
    face = face.reshape(devcount, 4, E_DEV).transpose(1, 0, 2).reshape(4, devcount * E_DEV)
    return (send_elements, send_faces, source.astype(jnp.int32), face.astype(jnp.int32))


def draw_send_elements(key, part):
    return graph_parts(key)[0]


def draw_send_faces(key, part):
    return graph_parts(key)[1]


def draw_neighbor_source(key, part):
    return graph_parts(key)[2]


def draw_neighbor_face(key, part):
    return graph_parts(key)[3]


def with_ends(array, stream_key, low, top_value):
    longest = array.shape.index(max(array.shape))
    spots = []
    for shift in (0, 1):
        where = [jax.random.randint(jax.random.fold_in(stream_key, axis), (), 0, length) for axis, length in enumerate(array.shape)]
        where[longest] = (where[longest] + shift) % array.shape[longest]
        spots.append(tuple(where))
    return array.at[spots[0]].set(low).at[spots[1]].set(top_value)


def block_levels(key, shape, cuts, low, top_value):
    factor_of = 1.0
    for position, shards_of in cuts:
        steps = jax.random.uniform(jax.random.fold_in(jax.random.fold_in(key, 6), position), (shards_of,), jnp.float32, low / len(cuts), top_value / len(cuts))
        factor_of = factor_of * jnp.repeat(jnp.exp(steps), shape[position] // shards_of).reshape((-1,) + (1,) * (len(shape) - 1 - position))
    return factor_of


def bell_draw(key, shape, deviation, bound, shards=(), held_as=jnp.bfloat16):
    result = deviation * jax.random.normal(key, shape, jnp.float32)
    if shards:
        result = result * block_levels(key, shape, shards, -0.22, 0.18)
    return jnp.clip(result, -bound, bound).astype(held_as)


def setup_inputs(seed: int = 0) -> dict:
    key_list = jax.random.split(jax.random.key(seed), 16)
    return {
        "state": bell_draw(key_list[0], (NQ, NB, ELEMENTS), 1.0, 6.0, ((2, 32),), jnp.float32),
        "ck_matrices": bell_draw(key_list[1], (3, NB, NB), 0.365, 2.0, (), jnp.float32),
        "vol_matrices": bell_draw(key_list[2], (3, NB, NB), NB ** -0.5, 0.5, (), jnp.float32),
        "face_project": bell_draw(key_list[3], (4, NFB, NB), NB ** -0.5, 0.5, (), jnp.float32),
        "face_lift": bell_draw(key_list[4], (4, NB, NFB), NFB ** -0.5, 1.0, (), jnp.float32),
        "face_turn": bell_draw(key_list[5], (3, NFB, NFB), NFB ** -0.5, 1.0, (), jnp.float32),
        "star_matrices": bell_draw(key_list[6], (3, NQ, NQ, ELEMENTS), 0.12, 0.75, ((3, 32),), jnp.float32),
        "flux_local": bell_draw(key_list[7], (4, NQ, NQ, ELEMENTS), 0.12, 0.75, ((3, 32),), jnp.float32),
        "flux_neighbor": bell_draw(key_list[8], (4, NQ, NQ, ELEMENTS), 0.12, 0.75, ((3, 32),), jnp.float32),
        "cluster": with_ends(jax.random.randint(key_list[9], (ELEMENTS,), 0, 3), jax.random.fold_in(key_list[9], 1), 0, 2).astype(jnp.int32),
        "send_elements": draw_send_elements(jax.random.fold_in(key_list[15], 71), 0),
        "send_faces": draw_send_faces(jax.random.fold_in(key_list[15], 71), 0),
        "neighbor_source": draw_neighbor_source(jax.random.fold_in(key_list[15], 71), 0),
        "neighbor_face": draw_neighbor_face(jax.random.fold_in(key_list[15], 71), 0),
        "neighbor_turn": with_ends(jax.random.randint(key_list[14], (4, ELEMENTS), 0, 3), jax.random.fold_in(key_list[14], 1), 0, 2).astype(jnp.int32),
    }


highest = lax.Precision.HIGHEST


def sub_lengths(cluster):
    return jnp.where(cluster == 0, 4, jnp.where(cluster == 1, 2, 1)).astype(jnp.int32)


def ck_step(deriv, ck_matrices, star_matrices):
    scaled = jnp.einsum('dpqe,qbe->dpbe', star_matrices, deriv, precision=highest)
    return jnp.einsum('dab,dpbe->pae', ck_matrices, scaled, precision=highest)


def predict(state, ck_matrices, star_matrices, lengths):
    duration = lengths.astype(jnp.float32) * 0.25
    own = jnp.zeros_like(state)
    fine = [jnp.zeros_like(state) for window in range(4)]
    deriv = state
    factorial = 1.0
    for order in range(ORDER):
        factorial = factorial * (order + 1)
        own = own + (duration ** (order + 1) / factorial)[None, None, :] * deriv
        for window in range(4):
            lower = window * 0.25
            upper = (window + 1) * 0.25
            coeff = (upper ** (order + 1) - lower ** (order + 1)) / factorial
            fine[window] = fine[window] + coeff * deriv
        if order + 1 < ORDER:
            deriv = ck_step(deriv, ck_matrices, star_matrices)
    return own, jnp.stack(fine)


def orient_faces(faces, neighbor_turn, face_turn):
    total = jnp.zeros_like(faces)
    for turn in range(3):
        turned = jnp.einsum('fg,iqge->iqfe', face_turn[turn], faces, precision=highest)
        total = total + jnp.where((neighbor_turn == turn)[:, None, None, :], turned, 0.0)
    return total


def correct(state, own, accum, vol_matrices, star_matrices, face_project, face_lift, flux_local, flux_neighbor):
    scaled = jnp.einsum('dpqe,qbe->dpbe', star_matrices, own, precision=highest)
    volume = jnp.einsum('dab,dpbe->pae', vol_matrices, scaled, precision=highest)
    on_face = jnp.einsum('ifb,qbe->iqfe', face_project, own, precision=highest)
    local_part = jnp.einsum('ipqe,iqfe->ipfe', flux_local, on_face, precision=highest)
    remote_part = jnp.einsum('ipqe,iqfe->ipfe', flux_neighbor, accum, precision=highest)
    lifted = jnp.einsum('ibf,ipfe->pbe', face_lift, local_part + remote_part, precision=highest)
    return state + volume - lifted


def reference(state, ck_matrices, vol_matrices, face_project, face_lift, face_turn, star_matrices, flux_local, flux_neighbor, cluster, send_elements, send_faces, neighbor_source, neighbor_face, neighbor_turn):
    devcount = N_DOM * N_SUB
    device_ids = jnp.arange(devcount, dtype=jnp.int32).reshape(N_DOM, N_SUB)
    directions = ((0, 1), (0, -1), (1, 1), (1, -1), (1, 2), (1, -2))
    columns = []
    facings = []
    for place in range(6):
        axis_number, offset = directions[place]
        senders = jnp.roll(device_ids, offset, axis=axis_number)
        listed = jnp.roll(send_elements[:, :, place, :], offset, axis=axis_number)
        columns.append(senders[:, :, None] * E_DEV + listed)
        facings.append(jnp.roll(send_faces[:, :, place, :], offset, axis=axis_number))
    slot_columns = jnp.stack(columns, axis=2).reshape(devcount, 6 * SLOT).astype(jnp.int32)
    slot_faces = jnp.stack(facings, axis=2).reshape(devcount, 6 * SLOT).astype(jnp.int32)
    source = neighbor_source.reshape(4, devcount, E_DEV)
    owner = jnp.arange(devcount, dtype=jnp.int32)[None, :, None]
    remote_slot = jnp.clip(source - E_DEV, 0, 6 * SLOT - 1).astype(jnp.int32)
    remote_column = slot_columns[owner, remote_slot]
    remote_facing = slot_faces[owner, remote_slot]
    global_column = jnp.where(source < E_DEV, owner * E_DEV + source, remote_column).reshape(4, ELEMENTS)
    face_used = jnp.where(source < E_DEV, neighbor_face.reshape(4, devcount, E_DEV), remote_facing).reshape(4, ELEMENTS)
    index = (face_used * ELEMENTS + global_column).astype(jnp.int32).reshape(-1)
    lengths = sub_lengths(cluster)
    own = jnp.zeros_like(state)
    fine = jnp.zeros((4,) + state.shape, jnp.float32)
    accum = jnp.zeros((4, NQ, NFB, ELEMENTS), jnp.float32)
    for substep in range(SUBSTEPS):
        phase = substep % lengths
        starting = phase == 0
        new_own, new_fine = predict(state, ck_matrices, star_matrices, lengths)
        own = jnp.where(starting[None, None, :], new_own, own)
        fine = jnp.where(starting[None, None, None, :], new_fine, fine)
        current = jnp.zeros_like(state)
        for window in range(4):
            current = current + jnp.where((phase == window)[None, None, :], fine[window], 0.0)
        projected = jnp.einsum('jfb,qbe->qfje', face_project, current, precision=highest)
        flat = projected.reshape(NQ, NFB, 4 * ELEMENTS)
        gathered = jnp.take(flat, index, axis=2).reshape(NQ, NFB, 4, ELEMENTS).transpose(2, 0, 1, 3)
        accum = accum + orient_faces(gathered, neighbor_turn, face_turn)
        ending = (phase + 1) == lengths
        updated = correct(state, own, accum, vol_matrices, star_matrices, face_project, face_lift, flux_local, flux_neighbor)
        state = jnp.where(ending[None, None, :], updated, state)
        accum = jnp.where(ending[None, None, None, :], 0.0, accum)
    return state
```

```python
import functools
import math

import jax
import jax.numpy as jnp
import numpy as np
from jax import lax
from jax.experimental import pallas as pl
from jax.experimental.pallas import tpu as pltpu
from jax.sharding import PartitionSpec as P

ORDER = 8
SUBSTEPS = 4
LANES = 128
HALF = 64

MESH = pl.DeviceIdType.MESH
f32 = jnp.float32
bf16 = jnp.bfloat16
highest = lax.Precision.HIGHEST


def split(x):
    high = x.astype(bf16)
    low = (x - high.astype(f32)).astype(bf16)
    return high, low


def three(x):
    high, low = split(x)
    return jnp.concatenate([high, low, high], axis=1)


def dot(a, b):
    return jnp.dot(a, b, preferred_element_type=f32)


def kernel(
    n_dom, n_sub, nq, ne, nb, nf,
    state_hbm, ck_hbm, vol_hbm, proj_hbm, lift_hbm, turn_hbm, star_hbm, local_hbm, far_hbm,
    cluster_hbm, elements_hbm, faces_hbm, source_hbm, face_hbm, orient_hbm,
    out_ref,
    state_ref, ck_ref, vol_ref, proj_ref, lift_ref, turn_ref, star_ref, local_ref, far_ref,
    cluster_ref, elements_ref, faces_ref, source_ref, face_ref, orient_ref, in_sem,
    pad, lines, columns, lines_misc, send_hot, w_ck, w_own, w_proj, w_lift,
    table_lhs, star_table, local_table, far_table,
    val, xs, halfx, own_ref, cur_ref, loc_ref, acc_ref, take_loc, take_rem, take_send,
    sbuf, rbuf, send_sem, recv_sem,
):
    rows = nq * ne
    dom = lax.axis_index("dom")
    sub = lax.axis_index("sub")
    has_prev = dom > 0
    has_next = dom < n_dom - 1
    targets = [
        (dom + 1, sub),
        (dom - 1, sub),
        (dom, lax.rem(sub + 1, n_sub)),
        (dom, lax.rem(sub + n_sub - 1, n_sub)),
        (dom, lax.rem(sub + 2, n_sub)),
        (dom, lax.rem(sub + n_sub - 2, n_sub)),
    ]
    sends = [has_next, has_prev, None, None, None, None]
    arrives = [has_prev, has_next, None, None, None, None]

    barrier = pltpu.get_barrier_semaphore()

    def guarded(flag, action):
        if flag is None:
            action()
        else:
            pl.when(flag)(action)

    for place in range(6):
        guarded(
            sends[place],
            lambda place=place: pl.semaphore_signal(
                barrier, inc=1, device_id=targets[place], device_id_type=MESH
            ),
        )

    from_refs = [
        star_hbm, ck_hbm, state_hbm, local_hbm, far_hbm, cluster_hbm, elements_hbm, faces_hbm,
        source_hbm, face_hbm, orient_hbm, proj_hbm, lift_hbm, turn_hbm, vol_hbm,
    ]
    to_refs = [
        star_ref, ck_ref, state_ref, local_ref, far_ref, cluster_ref, elements_ref, faces_ref,
        source_ref, face_ref, orient_ref, proj_ref, lift_ref, turn_ref, vol_ref,
    ]
    loads = [
        pltpu.make_async_copy(from_refs[k], to_refs[k], in_sem.at[k]) for k in range(len(to_refs))
    ]
    for load in loads:
        load.start()

    lane = lax.broadcasted_iota(jnp.int32, (ne, LANES), 1)
    left = lane < HALF
    lane_mod = lane & (HALF - 1)

    @pl.when(dom == 0)
    def _():
        rbuf[:, 0] = jnp.zeros(rbuf.shape[0:1] + rbuf.shape[2:], f32)

    @pl.when(dom == n_dom - 1)
    def _():
        rbuf[:, 1] = jnp.zeros(rbuf.shape[0:1] + rbuf.shape[2:], f32)

    pad[...] = jnp.zeros_like(pad)
    lines[...] = jnp.zeros_like(lines)
    lines_misc[...] = jnp.zeros_like(lines_misc)
    val[...] = jnp.zeros_like(val)
    acc_ref[...] = jnp.zeros_like(acc_ref)
    for load in loads:
        load.wait()

    for p in range(nq):
        for q in range(nq):
            lines[p, q * 3 : q * 3 + 3, 0:ne] = star_ref[p, q]
            lines[p, 32 + q * 4 : 36 + q * 4, 0:ne] = -local_ref[p, q]
            lines[p, 72 + q * 4 : 76 + q * 4, 0:ne] = -far_ref[p, q]
    for p in range(nq):
        columns[p] = jnp.transpose(lines[p])[0:ne]

    halves = split(columns[...].reshape(rows, LANES))
    table_lhs[...] = jnp.concatenate(halves, axis=0)
    pick = lax.broadcasted_iota(jnp.int32, (LANES, LANES), 0)
    left_pick = lax.broadcasted_iota(jnp.int32, (LANES, LANES), 1) < HALF

    def spread(hots, depth):
        both = dot(table_lhs[:, 0:depth], jnp.concatenate(hots, axis=1))
        return both[0:rows] + both[rows : 2 * rows]

    def one_hot(j, depth):
        return jnp.where(pick[0:depth] == j, 1.0, 0.0).astype(bf16)

    for j in range(0, 3 * nq, 2):
        pair = spread([one_hot(j, 32), one_hot(j + 1, 32)], 32)
        star_table[j] = pair[:, 0:LANES]
        star_table[j + 1] = pair[:, LANES : 2 * LANES]

    def fill_flux():
        for j in range(0, 4 * nq, 2):
            pair = spread([one_hot(32 + j, LANES), one_hot(33 + j, LANES)], LANES)
            local_table[j] = pair[:, 0:LANES]
            local_table[j + 1] = pair[:, LANES : 2 * LANES]
        for q in range(nq):
            hots = []
            for side in range(2):
                j = 72 + q * 4 + 2 * side
                hots.append(
                    jnp.where(pick == jnp.where(left_pick, j, j + 1), 1.0, 0.0).astype(bf16)
                )
            far_table[q] = spread(hots, LANES)

    def place_weight(weight, slot, column):
        high, low = split(jnp.transpose(pad[slot]))
        where = slice(column * LANES, (column + 1) * LANES)
        weight[0:LANES, where] = high
        weight[LANES : 2 * LANES, where] = high
        weight[2 * LANES : 3 * LANES, where] = low

    depth = 3 * 4 * HALF
    for d in range(3):
        pad[d, 0:nb, 0:nb] = ck_ref[d]
        place_weight(w_ck, d, d)
    for i in range(4):
        pad[10 + i, 0:nf, 0:nb] = proj_ref[:, i]
        pad[10 + i, HALF : HALF + nf, 0:nb] = proj_ref[:, i]
        place_weight(w_proj, 10 + i, i)

    def later_weights():
        for d in range(3):
            pad[3 + d, 0:nb, 0:nb] = vol_ref[d]
        for i in range(4):
            pad[6 + i, 0:nb, 0:nf] = jnp.transpose(lift_ref[:, i])
            lift = pad[6 + i][:, 0:nf]
            for h in range(3):
                pad[14 + h * 4 + i, :, 0:nf] = jnp.dot(
                    lift, turn_ref[h], precision=highest, preferred_element_type=f32
                )
            pad[26 + i, :, 0:nb] = jnp.dot(
                lift, proj_ref[:, i], precision=highest, preferred_element_type=f32
            )
        for d in range(3):
            place_weight(w_own, 3 + d, d)
        for i in range(4):
            place_weight(w_own, 26 + i, 3 + i)
        for h in range(3):
            for i in range(4):
                high, low = split(jnp.transpose(pad[14 + h * 4 + i])[0:HALF])
                start = (h * 4 + i) * HALF
                w_lift[start : start + HALF, :] = high
                w_lift[depth + start : depth + start + HALF, :] = high
                w_lift[2 * depth + start : 2 * depth + start + HALF, :] = low

    source = source_ref[...]
    is_local = source < ne
    slot = source - ne
    lines_misc[0:1, 0:ne] = cluster_ref[...].astype(f32)
    lines_misc[8:12, 0:ne] = orient_ref[...].astype(f32)
    lines_misc[16:20, 0:ne] = jnp.where(is_local, face_ref[...] * ne + source, 1000).astype(f32)
    lines_misc[24:28, 0:ne] = jnp.where(is_local, 1000, slot + 4 * (slot >> 2)).astype(f32)
    misc = jnp.transpose(lines_misc[...])[0:ne].astype(jnp.int32)

    def column(c):
        return jnp.broadcast_to(misc[:, c : c + 1], (ne, LANES))

    def chosen(index):
        return jnp.where(lane_mod == index, 1.0, 0.0).astype(bf16)

    cluster = column(0)
    lengths = jnp.where(cluster == 0, 4, jnp.where(cluster == 1, 2, 1))
    turns = [
        jnp.where(left, column(8 + 2 * side), column(9 + 2 * side)) for side in range(2)
    ]
    turn_wide = jnp.concatenate(turns, axis=1)
    for i in range(4):
        take_loc[i * ne : (i + 1) * ne, :] = chosen(column(16 + i))
        take_rem[0, i * ne : (i + 1) * ne, :] = chosen(column(24 + i))
        take_rem[1, i * ne : (i + 1) * ne, :] = chosen(column(24 + i) + 4)
    send_index = faces_ref[...] * ne + elements_ref[...]
    for d in range(6):
        hot = jnp.where(
            lane_mod[0:4] == jnp.broadcast_to(send_index[:, d : d + 1], (4, LANES)), 1.0, 0.0
        )
        send_hot[d * 8 : d * 8 + 4, :] = hot
        send_hot[d * 8 + 4 : d * 8 + 8, :] = hot
    take_send[...] = send_hot[...].astype(bf16)

    for q in range(nq):
        val[q * ne : (q + 1) * ne, 0:nb] = state_ref[q]

    greeted = 4 + has_prev.astype(jnp.int32) + has_next.astype(jnp.int32)

    upper_rows = (lax.broadcasted_iota(jnp.int32, (48, LANES), 0) & 7) < 4
    left48 = lax.broadcasted_iota(jnp.int32, (48, LANES), 1) < HALF

    def copy_of(s, place):
        return pltpu.make_async_remote_copy(
            src_ref=sbuf.at[s, place],
            dst_ref=rbuf.at[s, place],
            send_sem=send_sem.at[s, place],
            recv_sem=recv_sem.at[s, place],
            device_id=targets[place],
            device_id_type=MESH,
        )

    def apply(x_ref, table, matrices, first, total):
        for d in range(matrices):
            for q in range(nq):
                lanes = slice((first + d) * LANES, (first + d + 1) * LANES)
                term = table[q * matrices + d].reshape(nq, ne, LANES) * x_ref[q * ne : (q + 1) * ne, lanes][None]
                total = term if total is None else total + term
        return total

    def substep(s, carry):
        phase = s & (lengths - 1)
        ending = phase + 1 == lengths
        factorial = 1.0
        groups = [slice(start, start + 8) for start in range(0, ne, 8)]
        whole = val[...].reshape(nq, ne, LANES)
        derivs = [whole[:, group] for group in groups]
        for order in range(ORDER):
            factorial = factorial * (order + 1)
            w_full = jnp.where(
                cluster == 0,
                np.float32(1.0 / factorial),
                jnp.where(
                    cluster == 1,
                    np.float32(0.5 ** (order + 1) / factorial),
                    np.float32(0.25 ** (order + 1) / factorial),
                ),
            )
            coeffs = [
                np.float32((((w + 1) * 0.25) ** (order + 1) - (w * 0.25) ** (order + 1)) / factorial)
                for w in range(4)
            ]
            w_now = jnp.where(
                phase == 0,
                coeffs[0],
                jnp.where(phase == 1, coeffs[1], jnp.where(phase == 2, coeffs[2], coeffs[3])),
            )
            for group, deriv in zip(groups, derivs):
                if order == 0:
                    own_ref[:, group, :] = w_full[group][None] * deriv
                    cur_ref[:, group, :] = w_now[group][None] * deriv
                else:
                    own_ref[:, group, :] += w_full[group][None] * deriv
                    cur_ref[:, group, :] += w_now[group][None] * deriv
            if order + 1 < ORDER:
                for g, deriv in enumerate(derivs):
                    halfx[g] = dot(three(deriv.reshape(nq * 8, LANES)), w_ck[...])
                derivs = []
                for g, group in enumerate(groups):
                    total = None
                    for d in range(3):
                        lanes = slice(d * LANES, (d + 1) * LANES)
                        for q in range(nq):
                            table = star_table[q * 3 + d].reshape(nq, ne, LANES)[:, group]
                            term = table * halfx[g, q * 8 : (q + 1) * 8, lanes][None]
                            total = term if total is None else total + term
                    derivs.append(total)

        faces = dot(three(cur_ref[...].reshape(rows, LANES)), w_proj[...])
        side_by_side = jnp.concatenate(
            [
                jnp.concatenate(
                    [faces[q * ne : (q + 1) * ne, j * LANES : (j + 1) * LANES] for j in range(4)],
                    axis=0,
                )
                for q in range(nq)
            ],
            axis=1,
        )
        stacked = jnp.concatenate(split(side_by_side), axis=0)
        outgoing = dot(take_send[...], stacked)
        pieces = [outgoing[:, q * LANES : (q + 1) * LANES] for q in range(nq)]
        packed = [
            jnp.where(left48, pieces[2 * t], pieces[2 * t + 1]) if 2 * t + 1 < nq
            else jnp.where(left48, pieces[2 * t], 0.0)
            for t in range((nq + 1) // 2)
        ]
        packed.append(jnp.zeros_like(packed[0]))
        for u in range(3):
            payload = jnp.where(upper_rows, packed[u], packed[u + 3])
            sbuf[s, :, :, u * LANES : (u + 1) * LANES] = payload.reshape(6, 8, LANES)
        @pl.when(s == 0)
        def _():
            pl.semaphore_wait(barrier, greeted)

        for place in (0, 1, 4, 5, 2, 3):
            guarded(sends[place], lambda place=place: copy_of(s, place).start())

        @pl.when(s == 0)
        def _():
            later_weights()
            fill_flux()

        acc_ref[...] += dot(take_loc[...], stacked)
        xs[...] = dot(three(own_ref[...].reshape(rows, LANES)), w_own[...])
        loc_ref[...] = apply(xs, local_table, 4, 3, apply(xs, star_table, 3, 0, None))

        for place in range(6):
            guarded(arrives[place], lambda place=place: copy_of(s, place).wait_recv())
        doubled = []
        for u in range(3):
            tile = rbuf[s, :, :, u * LANES : (u + 1) * LANES].reshape(48, LANES)
            turned = pltpu.roll(tile, HALF, 1)
            doubled.append(jnp.where(left48, tile, turned))
            doubled.append(jnp.where(left48, turned, tile))
        arrived = jnp.concatenate(doubled, axis=1)
        high, low = split(arrived)
        blank = jnp.zeros((16, 6 * LANES), bf16)
        arrived = jnp.concatenate([high, blank, low, blank], axis=0)
        acc_ref[:, 0 : 6 * LANES] += dot(take_rem[0], arrived)
        acc_ref[:, 6 * LANES :] += dot(take_rem[1], arrived[:, 0 : 3 * LANES])

        total = None
        for q in range(nq):
            where = slice(q * LANES, (q + 1) * LANES)
            sides = [
                jnp.where(
                    left,
                    acc_ref[2 * side * ne : (2 * side + 1) * ne, where],
                    acc_ref[(2 * side + 1) * ne : (2 * side + 2) * ne, where],
                )
                for side in range(2)
            ]
            wide = jnp.concatenate(sides, axis=1)
            term = far_table[q].reshape(nq, ne, 2 * LANES) * wide[None]
            total = term if total is None else total + term
        masked = jnp.concatenate(
            [
                jnp.where((turn_wide == h)[None], total, 0.0).reshape(rows, 2 * LANES)
                for h in range(3)
            ],
            axis=1,
        )
        upd = dot(three(masked), w_lift[...]).reshape(nq, ne, LANES) + loc_ref[...]
        old = val[...].reshape(nq, ne, LANES)
        val[...] = jnp.where(ending[None], old + upd, old).reshape(rows, LANES)
        for i in range(4):
            for q in range(nq):
                where = slice(q * LANES, (q + 1) * LANES)
                here = slice(i * ne, (i + 1) * ne)
                acc_ref[here, where] = jnp.where(ending, 0.0, acc_ref[here, where])
        return carry

    lax.fori_loop(0, SUBSTEPS, substep, 0)
    out_ref[...] = val[...].reshape(nq, ne, LANES)

    def drain(s, carry):
        for place in range(6):
            guarded(sends[place], lambda place=place: copy_of(s, place).wait_send())
        return carry

    lax.fori_loop(0, SUBSTEPS, drain, 0)


def shards(
    n_dom, n_sub,
    state, ck_matrices, vol_matrices, face_project, face_lift, face_turn,
    star_matrices, flux_local, flux_neighbor, cluster,
    send_elements, send_faces, neighbor_source, neighbor_face, neighbor_turn,
):
    nq, nb, ne = state.shape
    nf = face_project.shape[1]
    rows = nq * ne
    operands = [
        state.transpose(0, 2, 1),
        ck_matrices,
        vol_matrices,
        face_project.transpose(1, 0, 2),
        face_lift.transpose(2, 0, 1),
        face_turn,
        star_matrices.transpose(1, 2, 0, 3),
        flux_local.transpose(1, 2, 0, 3),
        flux_neighbor.transpose(1, 2, 0, 3),
        cluster[None],
        send_elements[0, 0].T,
        send_faces[0, 0].T,
        neighbor_source,
        neighbor_face,
        neighbor_turn,
    ]
    whole = pl.BlockSpec(memory_space=pltpu.VMEM)
    result = pl.pallas_call(
        functools.partial(kernel, n_dom, n_sub, nq, ne, nb, nf),
        out_shape=pltpu.VMEM((nq, ne, LANES), f32),
        in_specs=[pl.BlockSpec(memory_space=pltpu.HBM)] * len(operands),
        out_specs=whole,
        scratch_shapes=[
            *[pltpu.VMEM(x.shape, x.dtype) for x in operands],
            pltpu.SemaphoreType.DMA((len(operands),)),
            pltpu.VMEM((30, LANES, LANES), f32),
            pltpu.VMEM((nq, LANES, LANES), f32),
            pltpu.VMEM((nq, ne, LANES), f32),
            pltpu.VMEM((32, LANES), f32),
            pltpu.VMEM((48, LANES), f32),
            pltpu.VMEM((3 * LANES, 3 * LANES), bf16),
            pltpu.VMEM((3 * LANES, 7 * LANES), bf16),
            pltpu.VMEM((3 * LANES, 4 * LANES), bf16),
            pltpu.VMEM((3 * 3 * 4 * HALF, LANES), bf16),
            pltpu.VMEM((2 * rows, LANES), bf16),
            pltpu.VMEM((3 * nq + 1, rows, LANES), f32),
            pltpu.VMEM((4 * nq, rows, LANES), f32),
            pltpu.VMEM((nq, rows, 2 * LANES), f32),
            pltpu.VMEM((rows, LANES), f32),
            pltpu.VMEM((rows, 7 * LANES), f32),
            pltpu.VMEM((ne // 8, nq * 8, 3 * LANES), f32),
            pltpu.VMEM((nq, ne, LANES), f32),
            pltpu.VMEM((nq, ne, LANES), f32),
            pltpu.VMEM((nq, ne, LANES), f32),
            pltpu.VMEM((4 * ne, nq * LANES), f32),
            pltpu.VMEM((4 * ne, LANES), bf16),
            pltpu.VMEM((2, 4 * ne, LANES), bf16),
            pltpu.VMEM((3 * ne, LANES), bf16),
            pltpu.VMEM((SUBSTEPS, 6, 8, 3 * LANES), f32),
            pltpu.VMEM((SUBSTEPS, 6, 8, 3 * LANES), f32),
            pltpu.SemaphoreType.DMA((SUBSTEPS, 6)),
            pltpu.SemaphoreType.DMA((SUBSTEPS, 6)),
        ],
        compiler_params=pltpu.CompilerParams(
            collective_id=0, has_side_effects=True, vmem_limit_bytes=24 * 1024 * 1024
        ),
    )(*[pltpu.with_memory_space_constraint(x, pltpu.HBM) for x in operands])
    return result[:, :, 0:nb].transpose(0, 2, 1)


def solution(mesh):
    both = ("dom", "sub")
    in_specs = (
        P(None, None, both),
        P(),
        P(),
        P(),
        P(),
        P(),
        P(None, None, None, both),
        P(None, None, None, both),
        P(None, None, None, both),
        P(both),
        P("dom", "sub", None, None),
        P("dom", "sub", None, None),
        P(None, both),
        P(None, both),
        P(None, both),
    )
    return jax.shard_map(
        functools.partial(shards, mesh.shape["dom"], mesh.shape["sub"]),
        mesh=mesh,
        in_specs=in_specs,
        out_specs=P(None, None, both),
        check_vma=False,
    )
```

```python
import functools
import math

import jax
import jax.numpy as jnp
import numpy as np
from jax import lax
from jax.experimental import pallas as pl
from jax.experimental.pallas import tpu as pltpu
from jax.sharding import PartitionSpec as P

ORDER = 8
SUBSTEPS = 4
LANES = 128
HALF = 64
THIRD = 40

MESH = pl.DeviceIdType.MESH
f32 = jnp.float32
bf16 = jnp.bfloat16
highest = lax.Precision.HIGHEST


def split(x):
    high = x.astype(bf16)
    low = (x - high.astype(f32)).astype(bf16)
    return high, low


def three(x):
    high, low = split(x)
    return jnp.concatenate([high, low, high], axis=1)


def dot(a, b):
    return jnp.dot(a, b, preferred_element_type=f32)


def kernel(
    n_dom, n_sub, nq, ne, nb, nf,
    state_hbm, ck_hbm, vol_hbm, proj_hbm, lift_hbm, turn_hbm, star_hbm, local_hbm, far_hbm,
    cluster_hbm, elements_hbm, faces_hbm, source_hbm, face_hbm, orient_hbm,
    out_ref,
    state_ref, ck_ref, vol_ref, proj_ref, lift_ref, turn_ref, star_ref, local_ref, far_ref,
    cluster_ref, elements_ref, faces_ref, source_ref, face_ref, orient_ref, source_scalar, in_sem,
    pad, star_lines, lines, columns, lines_misc, w_ck, w_own, w_proj, w_lift,
    table_lhs, star_table, local_table, far_table,
    val, xs, halfx, own_ref, cur_ref, loc_ref, acc_ref, take_loc, turn_mask, face_rows, got_rows,
    send_row, take_row, sbuf, rbuf, arrived, send_sem, recv_sem,
):
    rows = nq * ne
    slots = elements_ref.shape[0]
    dom = lax.axis_index("dom")
    sub = lax.axis_index("sub")
    has_prev = dom > 0
    has_next = dom < n_dom - 1
    targets = [
        (dom + 1, sub),
        (dom - 1, sub),
        (dom, lax.rem(sub + 1, n_sub)),
        (dom, lax.rem(sub + n_sub - 1, n_sub)),
        (dom, lax.rem(sub + 2, n_sub)),
        (dom, lax.rem(sub + n_sub - 2, n_sub)),
    ]
    sends = [has_next, has_prev, None, None, None, None]
    arrives = [has_prev, has_next, None, None, None, None]

    barrier = pltpu.get_barrier_semaphore()

    def guarded(flag, action):
        if flag is None:
            action()
        else:
            pl.when(flag)(action)

    for place in range(6):
        guarded(
            sends[place],
            lambda place=place: pl.semaphore_signal(
                barrier, inc=1, device_id=targets[place], device_id_type=MESH
            ),
        )

    from_refs = [
        star_hbm, ck_hbm, state_hbm, local_hbm, far_hbm, cluster_hbm, elements_hbm, faces_hbm,
        source_hbm, face_hbm, orient_hbm, proj_hbm, lift_hbm, turn_hbm, vol_hbm, source_hbm,
    ]
    to_refs = [
        star_ref, ck_ref, state_ref, local_ref, far_ref, cluster_ref, elements_ref, faces_ref,
        source_ref, face_ref, orient_ref, proj_ref, lift_ref, turn_ref, vol_ref, source_scalar,
    ]
    loads = [
        pltpu.make_async_copy(from_refs[k], to_refs[k], in_sem.at[k]) for k in range(len(to_refs))
    ]
    for load in loads:
        load.start()

    lane = lax.broadcasted_iota(jnp.int32, (ne, LANES), 1)
    left = lane < HALF
    lane_mod = lane & (HALF - 1)

    @pl.when(dom == 0)
    def _():
        rbuf[:, 0:slots] = jnp.zeros((SUBSTEPS, slots, 4, LANES), f32)

    @pl.when(dom == n_dom - 1)
    def _():
        rbuf[:, slots : 2 * slots] = jnp.zeros((SUBSTEPS, slots, 4, LANES), f32)

    pad[...] = jnp.zeros_like(pad)
    star_lines[...] = jnp.zeros_like(star_lines)
    lines_misc[...] = jnp.zeros_like(lines_misc)
    val[...] = jnp.zeros_like(val)
    acc_ref[...] = jnp.zeros_like(acc_ref)
    face_rows[4 * rows :] = jnp.zeros((face_rows.shape[0] - 4 * rows, LANES), f32)
    arrived[6 * slots] = jnp.zeros((4, LANES), f32)
    for load in loads:
        load.wait()

    for p in range(nq):
        for q in range(nq):
            star_lines[p, q * 3 : q * 3 + 3, 0:ne] = star_ref[p, q]
    star_columns = [jnp.transpose(star_lines[p])[0:ne] for p in range(nq)]
    star_lhs = jnp.concatenate(split(jnp.concatenate(star_columns, axis=0)), axis=0)
    pick = lax.broadcasted_iota(jnp.int32, (LANES, LANES), 0)
    left_pick = lax.broadcasted_iota(jnp.int32, (LANES, LANES), 1) < HALF

    def spread(lhs, hots):
        both = dot(lhs, jnp.concatenate(hots, axis=1))
        return both[0:rows] + both[rows : 2 * rows]

    def one_hot(j, depth):
        return jnp.where(pick[0:depth] == j, 1.0, 0.0).astype(bf16)

    for j in range(0, 3 * nq, 2):
        pair = spread(star_lhs, [one_hot(j, 32), one_hot(j + 1, 32)])
        star_table[j] = pair[:, 0:LANES]
        star_table[j + 1] = pair[:, LANES : 2 * LANES]

    def fill_flux():
        lines[...] = jnp.zeros_like(lines)
        for p in range(nq):
            for q in range(nq):
                lines[p, q * 4 : q * 4 + 4, 0:ne] = -local_ref[p, q]
                lines[p, 4 * nq + q * 4 : 4 * nq + q * 4 + 4, 0:ne] = -far_ref[p, q]
        for p in range(nq):
            columns[p] = jnp.transpose(lines[p])[0:ne]
        table_lhs[...] = jnp.concatenate(split(columns[...].reshape(rows, 8 * nq)), axis=0)
        for j in range(0, 4 * nq, 2):
            pair = spread(table_lhs[...], [one_hot(j, 8 * nq), one_hot(j + 1, 8 * nq)])
            local_table[j] = pair[:, 0:LANES]
            local_table[j + 1] = pair[:, LANES : 2 * LANES]
        for q in range(nq):
            hots = []
            for side in range(2):
                j = 4 * nq + q * 4 + 2 * side
                hots.append(
                    jnp.where(pick[0 : 8 * nq] == jnp.where(left_pick[0 : 8 * nq], j, j + 1), 1.0, 0.0).astype(bf16)
                )
            far_table[q] = spread(table_lhs[...], hots)

    def place_weight(weight, slot, column):
        high, low = split(jnp.transpose(pad[slot]))
        where = slice(column * LANES, (column + 1) * LANES)
        weight[0:LANES, where] = high
        weight[LANES : 2 * LANES, where] = high
        weight[2 * LANES : 3 * LANES, where] = low

    depth = 3 * 4 * HALF
    for d in range(3):
        pad[d, 0:nb, 0:nb] = ck_ref[d]
        place_weight(w_ck, d, d)
    for i in range(4):
        pad[10 + i, 0:nf, 0:nb] = proj_ref[:, i]
        pad[10 + i, THIRD : THIRD + nf, 0:nb] = proj_ref[:, i]
        pad[10 + i, 2 * THIRD : 2 * THIRD + nf, 0:nb] = proj_ref[:, i]
        place_weight(w_proj, 10 + i, i)

    def later_weights():
        for d in range(3):
            pad[3 + d, 0:nb, 0:nb] = vol_ref[d]
            place_weight(w_own, 3 + d, d)
        pad[6:10] = jnp.zeros((4, LANES, LANES), f32)
        for i in range(4):
            pad[6 + i, 0:nf, 0:nb] = lift_ref[:, i]
        lifts = jnp.concatenate([pad[6 + i, 0:nf, :] for i in range(4)], axis=1)
        for h in range(3):
            turned = jnp.dot(
                jnp.transpose(turn_ref[h]), lifts, precision=highest, preferred_element_type=f32
            )
            for i in range(4):
                pad[14 + h * 4 + i, 0:nf, :] = turned[:, i * LANES : (i + 1) * LANES]
                high, low = split(pad[14 + h * 4 + i, 0:HALF, :])
                start = (h * 4 + i) * HALF
                w_lift[start : start + HALF, :] = high
                w_lift[depth + start : depth + start + HALF, :] = high
                w_lift[2 * depth + start : 2 * depth + start + HALF, :] = low
        for i in range(4):
            product = jnp.dot(
                jnp.transpose(proj_ref[:, i]), lifts[:, i * LANES : (i + 1) * LANES],
                precision=highest, preferred_element_type=f32,
            )
            pad[26 + i, 0:nb, :] = product
            high, low = split(pad[26 + i])
            where = slice((3 + i) * LANES, (4 + i) * LANES)
            w_own[0:LANES, where] = high
            w_own[LANES : 2 * LANES, where] = high
            w_own[2 * LANES : 3 * LANES, where] = low

    lines_misc[0:1, 0:ne] = cluster_ref[...].astype(f32)
    cluster = jnp.transpose(lines_misc[0:8])[0:ne].astype(jnp.int32)
    cluster = jnp.broadcast_to(cluster[:, 0:1], (ne, LANES))
    lengths = jnp.where(cluster == 0, 4, jnp.where(cluster == 1, 2, 1))

    def fill_choices():
        source = source_ref[...]
        is_local = source < ne
        lines_misc[8:12, 0:ne] = orient_ref[...].astype(f32)
        lines_misc[16:20, 0:ne] = jnp.where(is_local, face_ref[...] * ne + source, 1000).astype(f32)
        misc = jnp.transpose(lines_misc[...])[0:ne].astype(jnp.int32)

        def column(c):
            return jnp.broadcast_to(misc[:, c : c + 1], (ne, LANES))

        turns = [
            jnp.where(left, column(8 + 2 * side), column(9 + 2 * side)) for side in range(2)
        ]
        turn_wide = jnp.concatenate(turns, axis=1)
        for i in range(4):
            hot = jnp.where(lane_mod == column(16 + i), 1.0, 0.0)
            take_loc[i * ne : (i + 1) * ne, :] = hot.astype(bf16)
        for h in range(3):
            turn_mask[h] = jnp.where(turn_wide == h, 1.0, 0.0).astype(bf16)

    for d in range(6):
        for k in range(slots):
            send_row[d * slots + k] = faces_ref[k, d] * rows + elements_ref[k, d]

    def fill_take():
        for i in range(4):
            for e in range(ne):
                place = source_scalar[i, e] - ne
                take_row[i * ne + e] = jnp.where(place < 0, 6 * slots, place)

    for q in range(nq):
        val[q * ne : (q + 1) * ne, 0:nb] = state_ref[q]

    greeted = 4 + has_prev.astype(jnp.int32) + has_next.astype(jnp.int32)

    lane4 = lax.broadcasted_iota(jnp.int32, (4, LANES), 1)

    def copy_of(s, place):
        return pltpu.make_async_remote_copy(
            src_ref=sbuf.at[s, pl.ds(place * slots, slots)],
            dst_ref=rbuf.at[s, pl.ds(place * slots, slots)],
            send_sem=send_sem.at[s, place],
            recv_sem=recv_sem.at[s, place],
            device_id=targets[place],
            device_id_type=MESH,
        )

    def apply(x_ref, table, matrices, first, total):
        for d in range(matrices):
            for q in range(nq):
                lanes = slice((first + d) * LANES, (first + d + 1) * LANES)
                term = table[q * matrices + d].reshape(nq, ne, LANES) * x_ref[q * ne : (q + 1) * ne, lanes][None]
                total = term if total is None else total + term
        return total

    def substep(s, carry):
        phase = s & (lengths - 1)
        ending = phase + 1 == lengths
        factorial = 1.0
        groups = [slice(start, start + 8) for start in range(0, ne, 8)]
        whole = val[...].reshape(nq, ne, LANES)
        derivs = [whole[:, group] for group in groups]
        for order in range(ORDER):
            factorial = factorial * (order + 1)
            w_full = jnp.where(
                cluster == 0,
                np.float32(1.0 / factorial),
                jnp.where(
                    cluster == 1,
                    np.float32(0.5 ** (order + 1) / factorial),
                    np.float32(0.25 ** (order + 1) / factorial),
                ),
            )
            coeffs = [
                np.float32((((w + 1) * 0.25) ** (order + 1) - (w * 0.25) ** (order + 1)) / factorial)
                for w in range(4)
            ]
            w_now = jnp.where(
                phase == 0,
                coeffs[0],
                jnp.where(phase == 1, coeffs[1], jnp.where(phase == 2, coeffs[2], coeffs[3])),
            )
            for group, deriv in zip(groups, derivs):
                if order == 0:
                    own_ref[:, group, :] = w_full[group][None] * deriv
                    cur_ref[:, group, :] = w_now[group][None] * deriv
                else:
                    own_ref[:, group, :] += w_full[group][None] * deriv
                    cur_ref[:, group, :] += w_now[group][None] * deriv
            if order + 1 < ORDER:
                for g, deriv in enumerate(derivs):
                    halfx[g] = dot(three(deriv.reshape(nq * 8, LANES)), w_ck[...])
                derivs = []
                for g, group in enumerate(groups):
                    total = None
                    for d in range(3):
                        lanes = slice(d * LANES, (d + 1) * LANES)
                        for q in range(nq):
                            table = star_table[q * 3 + d].reshape(nq, ne, LANES)[:, group]
                            term = table * halfx[g, q * 8 : (q + 1) * 8, lanes][None]
                            total = term if total is None else total + term
                    derivs.append(total)

        for g, group in enumerate(groups):
            faces = dot(three(cur_ref[:, group, :].reshape(nq * 8, LANES)), w_proj[...])
            for j in range(4):
                for q in range(nq):
                    first = j * rows + q * ne + g * 8
                    face_rows[first : first + 8] = faces[q * 8 : (q + 1) * 8, j * LANES : (j + 1) * LANES]
        for slot in range(6 * slots):
            start = send_row[slot]
            parts = [face_rows[pl.ds(start + g * ne, 4, stride=3 * ne)] for g in range(3)]
            sbuf[s, slot] = jnp.where(
                lane4 < THIRD, parts[0], jnp.where(lane4 < 2 * THIRD, parts[1], parts[2])
            )

        @pl.when(s == 0)
        def _():
            pl.semaphore_wait(barrier, greeted)

        for place in (0, 1, 4, 5, 2, 3):
            guarded(sends[place], lambda place=place: copy_of(s, place).start())

        @pl.when(s == 0)
        def _():
            later_weights()
            fill_flux()
            fill_choices()
            fill_take()

        side_by_side = jnp.concatenate(
            [
                jnp.concatenate(
                    [face_rows[j * rows + q * ne : j * rows + (q + 1) * ne] for j in range(4)],
                    axis=0,
                )
                for q in range(nq)
            ],
            axis=1,
        )
        stacked = jnp.concatenate(split(side_by_side), axis=0)
        near = dot(take_loc[...], stacked)
        for q in range(nq):
            where = slice(q * LANES, (q + 1) * LANES)
            for side in range(2):
                acc_ref[q, :, side * LANES : (side + 1) * LANES] += jnp.where(
                    left,
                    near[2 * side * ne : (2 * side + 1) * ne, where],
                    pltpu.roll(near[(2 * side + 1) * ne : (2 * side + 2) * ne, where], HALF, 1),
                )
        xs[...] = dot(three(own_ref[...].reshape(rows, LANES)), w_own[...])
        loc_ref[...] = apply(xs, local_table, 4, 3, apply(xs, star_table, 3, 0, None))

        for place in range(6):
            guarded(arrives[place], lambda place=place: copy_of(s, place).wait_recv())
        arrived[0 : 6 * slots] = rbuf[s]
        for row in range(4 * ne):
            got_rows[pl.ds(row, 4, stride=4 * ne)] = arrived[take_row[row]]

        def got(t, i):
            return got_rows[(t * 4 + i) * ne : (t * 4 + i + 1) * ne]

        ending_wide = jnp.concatenate([ending, ending], axis=1)
        total = None
        for q in range(nq):
            t, g = divmod(q, 3)
            sides = []
            for side in range(2):
                first, second = got(t, 2 * side), got(t, 2 * side + 1)
                if g:
                    first = pltpu.roll(first, LANES - g * THIRD, 1)
                second = pltpu.roll(second, (HALF - g * THIRD) % LANES, 1)
                sides.append(jnp.where(left, first, second))
            wide = acc_ref[q] + jnp.concatenate(sides, axis=1)
            term = far_table[q].reshape(nq, ne, 2 * LANES) * wide[None]
            total = term if total is None else total + term
            acc_ref[q] = jnp.where(ending_wide, 0.0, wide)
        parts = [part.reshape(nq, ne, 2 * LANES) for part in split(total.reshape(rows, 2 * LANES))]
        high, low = [
            [(part * turn_mask[h][None]).reshape(rows, 2 * LANES) for h in range(3)] for part in parts
        ]
        masked = jnp.concatenate(high + low + high, axis=1)
        upd = dot(masked, w_lift[...]).reshape(nq, ne, LANES) + loc_ref[...]
        old = val[...].reshape(nq, ne, LANES)
        val[...] = jnp.where(ending[None], old + upd, old).reshape(rows, LANES)
        return carry

    lax.fori_loop(0, SUBSTEPS, substep, 0)
    out_ref[...] = val[...].reshape(nq, ne, LANES)

    def drain(s, carry):
        for place in range(6):
            guarded(sends[place], lambda place=place: copy_of(s, place).wait_send())
        return carry

    lax.fori_loop(0, SUBSTEPS, drain, 0)


def shards(
    n_dom, n_sub,
    state, ck_matrices, vol_matrices, face_project, face_lift, face_turn,
    star_matrices, flux_local, flux_neighbor, cluster,
    send_elements, send_faces, neighbor_source, neighbor_face, neighbor_turn,
):
    nq, nb, ne = state.shape
    nf = face_project.shape[1]
    rows = nq * ne
    slots = send_elements.shape[3]
    operands = [
        state.transpose(0, 2, 1),
        ck_matrices,
        vol_matrices,
        face_project.transpose(1, 0, 2),
        face_lift.transpose(2, 0, 1),
        face_turn,
        star_matrices.transpose(1, 2, 0, 3),
        flux_local.transpose(1, 2, 0, 3),
        flux_neighbor.transpose(1, 2, 0, 3),
        cluster[None],
        send_elements[0, 0].T,
        send_faces[0, 0].T,
        neighbor_source,
        neighbor_face,
        neighbor_turn,
    ]
    whole = pl.BlockSpec(memory_space=pltpu.VMEM)
    result = pl.pallas_call(
        functools.partial(kernel, n_dom, n_sub, nq, ne, nb, nf),
        out_shape=pltpu.VMEM((nq, ne, LANES), f32),
        in_specs=[pl.BlockSpec(memory_space=pltpu.HBM)] * len(operands),
        out_specs=whole,
        scratch_shapes=[
            *[(pltpu.SMEM if k in (10, 11) else pltpu.VMEM)(x.shape, x.dtype) for k, x in enumerate(operands)],
            pltpu.SMEM(neighbor_source.shape, jnp.int32),
            pltpu.SemaphoreType.DMA((len(operands) + 1,)),
            pltpu.VMEM((30, LANES, LANES), f32),
            pltpu.VMEM((nq, 32, LANES), f32),
            pltpu.VMEM((nq, 8 * nq, LANES), f32),
            pltpu.VMEM((nq, ne, 8 * nq), f32),
            pltpu.VMEM((32, LANES), f32),
            pltpu.VMEM((3 * LANES, 3 * LANES), bf16),
            pltpu.VMEM((3 * LANES, 7 * LANES), bf16),
            pltpu.VMEM((3 * LANES, 4 * LANES), bf16),
            pltpu.VMEM((3 * 3 * 4 * HALF, LANES), bf16),
            pltpu.VMEM((2 * rows, 8 * nq), bf16),
            pltpu.VMEM((3 * nq + 1, rows, LANES), f32),
            pltpu.VMEM((4 * nq, rows, LANES), f32),
            pltpu.VMEM((nq, rows, 2 * LANES), f32),
            pltpu.VMEM((rows, LANES), f32),
            pltpu.VMEM((rows, 7 * LANES), f32),
            pltpu.VMEM((ne // 8, nq * 8, 3 * LANES), f32),
            pltpu.VMEM((nq, ne, LANES), f32),
            pltpu.VMEM((nq, ne, LANES), f32),
            pltpu.VMEM((nq, ne, LANES), f32),
            pltpu.VMEM((nq, ne, 2 * LANES), f32),
            pltpu.VMEM((4 * ne, LANES), bf16),
            pltpu.VMEM((3, ne, 2 * LANES), bf16),
            pltpu.VMEM((4 * rows + 16 * ne, LANES), f32),
            pltpu.VMEM((4 * 4 * ne, LANES), f32),
            pltpu.SMEM((6 * slots,), jnp.int32),
            pltpu.SMEM((4 * ne,), jnp.int32),
            pltpu.VMEM((SUBSTEPS, 6 * slots, 4, LANES), f32),
            pltpu.VMEM((SUBSTEPS, 6 * slots, 4, LANES), f32),
            pltpu.VMEM((6 * slots + 1, 4, LANES), f32),
            pltpu.SemaphoreType.DMA((SUBSTEPS, 6)),
            pltpu.SemaphoreType.DMA((SUBSTEPS, 6)),
        ],
        compiler_params=pltpu.CompilerParams(
            collective_id=0, has_side_effects=True, vmem_limit_bytes=24 * 1024 * 1024
        ),
    )(*[pltpu.with_memory_space_constraint(x, pltpu.HBM) for x in operands])
    return result[:, :, 0:nb].transpose(0, 2, 1)


def solution(mesh):
    both = ("dom", "sub")
    in_specs = (
        P(None, None, both),
        P(),
        P(),
        P(),
        P(),
        P(),
        P(None, None, None, both),
        P(None, None, None, both),
        P(None, None, None, both),
        P(both),
        P("dom", "sub", None, None),
        P("dom", "sub", None, None),
        P(None, both),
        P(None, both),
        P(None, both),
    )
    return jax.shard_map(
        functools.partial(shards, mesh.shape["dom"], mesh.shape["sub"]),
        mesh=mesh,
        in_specs=in_specs,
        out_specs=P(None, None, both),
        check_vma=False,
    )
```

```python
import functools
import math

import jax
import jax.numpy as jnp
import numpy as np
from jax import lax
from jax.experimental import pallas as pl
from jax.experimental.pallas import tpu as pltpu
from jax.sharding import PartitionSpec as P

ORDER = 8
SUBSTEPS = 4
LANES = 128
HALF = 64
THIRD = 40

MESH = pl.DeviceIdType.MESH
f32 = jnp.float32
bf16 = jnp.bfloat16
highest = lax.Precision.HIGHEST


def split(x):
    high = x.astype(bf16)
    low = (x - high.astype(f32)).astype(bf16)
    return high, low


def three(x):
    high, low = split(x)
    return jnp.concatenate([high, low, high], axis=1)


def dot(a, b):
    return jnp.dot(a, b, preferred_element_type=f32)


def kernel(
    n_dom, n_sub, nq, ne, nb, nf,
    state_hbm, ck_hbm, vol_hbm, proj_hbm, lift_hbm, turn_hbm, star_hbm, local_hbm, far_hbm,
    cluster_hbm, elements_hbm, faces_hbm, source_hbm, face_hbm, orient_hbm,
    out_ref,
    state_ref, ck_ref, vol_ref, proj_ref, lift_ref, turn_ref, star_ref, local_ref, far_ref,
    cluster_ref, elements_ref, faces_ref, source_ref, face_ref, orient_ref, source_scalar, in_sem,
    pad, star_lines, lines, columns, lines_misc, w_ck, w_own, w_proj, w_lift,
    table_lhs, star_table, local_table, far_table,
    val, xs, halfx, series, cur_ref, loc_ref, acc_ref, take_loc, turn_mask, face_rows, got_rows,
    send_row, take_row, sbuf, rbuf, arrived, send_sem, recv_sem,
):
    rows = nq * ne
    slots = elements_ref.shape[0]
    dom = lax.axis_index("dom")
    sub = lax.axis_index("sub")
    has_prev = dom > 0
    has_next = dom < n_dom - 1
    targets = [
        (dom + 1, sub),
        (dom - 1, sub),
        (dom, lax.rem(sub + 1, n_sub)),
        (dom, lax.rem(sub + n_sub - 1, n_sub)),
        (dom, lax.rem(sub + 2, n_sub)),
        (dom, lax.rem(sub + n_sub - 2, n_sub)),
    ]
    sends = [has_next, has_prev, None, None, None, None]
    arrives = [has_prev, has_next, None, None, None, None]

    barrier = pltpu.get_barrier_semaphore()

    def guarded(flag, action):
        if flag is None:
            action()
        else:
            pl.when(flag)(action)

    for place in range(6):
        guarded(
            sends[place],
            lambda place=place: pl.semaphore_signal(
                barrier, inc=1, device_id=targets[place], device_id_type=MESH
            ),
        )

    from_refs = [
        star_hbm, ck_hbm, state_hbm, local_hbm, far_hbm, cluster_hbm, elements_hbm, faces_hbm,
        source_hbm, face_hbm, orient_hbm, proj_hbm, lift_hbm, turn_hbm, vol_hbm, source_hbm,
    ]
    to_refs = [
        star_ref, ck_ref, state_ref, local_ref, far_ref, cluster_ref, elements_ref, faces_ref,
        source_ref, face_ref, orient_ref, proj_ref, lift_ref, turn_ref, vol_ref, source_scalar,
    ]
    loads = [
        pltpu.make_async_copy(from_refs[k], to_refs[k], in_sem.at[k]) for k in range(len(to_refs))
    ]
    for load in loads:
        load.start()

    lane = lax.broadcasted_iota(jnp.int32, (ne, LANES), 1)
    left = lane < HALF
    lane_mod = lane & (HALF - 1)

    @pl.when(dom == 0)
    def _():
        rbuf[:, 0:slots] = jnp.zeros((SUBSTEPS, slots, 4, LANES), f32)

    @pl.when(dom == n_dom - 1)
    def _():
        rbuf[:, slots : 2 * slots] = jnp.zeros((SUBSTEPS, slots, 4, LANES), f32)

    pad[...] = jnp.zeros_like(pad)
    star_lines[...] = jnp.zeros_like(star_lines)
    lines_misc[...] = jnp.zeros_like(lines_misc)
    val[...] = jnp.zeros_like(val)
    acc_ref[...] = jnp.zeros_like(acc_ref)
    face_rows[4 * rows :] = jnp.zeros((face_rows.shape[0] - 4 * rows, LANES), f32)
    arrived[6 * slots] = jnp.zeros((4, LANES), f32)
    for load in loads:
        load.wait()

    for p in range(nq):
        for q in range(nq):
            star_lines[p, q * 3 : q * 3 + 3, 0:ne] = star_ref[p, q]
    star_columns = [jnp.transpose(star_lines[p])[0:ne] for p in range(nq)]
    star_lhs = jnp.concatenate(split(jnp.concatenate(star_columns, axis=0)), axis=0)
    pick = lax.broadcasted_iota(jnp.int32, (LANES, LANES), 0)
    left_pick = lax.broadcasted_iota(jnp.int32, (LANES, LANES), 1) < HALF

    def spread(lhs, hots):
        both = dot(lhs, jnp.concatenate(hots, axis=1))
        return both[0:rows] + both[rows : 2 * rows]

    def one_hot(j, depth):
        return jnp.where(pick[0:depth] == j, 1.0, 0.0).astype(bf16)

    for j in range(0, 3 * nq, 2):
        pair = spread(star_lhs, [one_hot(j, 32), one_hot(j + 1, 32)])
        star_table[j] = pair[:, 0:LANES]
        star_table[j + 1] = pair[:, LANES : 2 * LANES]

    def fill_flux():
        lines[...] = jnp.zeros_like(lines)
        for p in range(nq):
            for q in range(nq):
                lines[p, q * 4 : q * 4 + 4, 0:ne] = -local_ref[p, q]
                lines[p, 4 * nq + q * 4 : 4 * nq + q * 4 + 4, 0:ne] = -far_ref[p, q]
        for p in range(nq):
            columns[p] = jnp.transpose(lines[p])[0:ne]
        table_lhs[...] = jnp.concatenate(split(columns[...].reshape(rows, 8 * nq)), axis=0)
        for j in range(0, 4 * nq, 2):
            pair = spread(table_lhs[...], [one_hot(j, 8 * nq), one_hot(j + 1, 8 * nq)])
            local_table[j] = pair[:, 0:LANES]
            local_table[j + 1] = pair[:, LANES : 2 * LANES]
        for q in range(nq):
            hots = []
            for side in range(2):
                j = 4 * nq + q * 4 + 2 * side
                hots.append(
                    jnp.where(pick[0 : 8 * nq] == jnp.where(left_pick[0 : 8 * nq], j, j + 1), 1.0, 0.0).astype(bf16)
                )
            far_table[q] = spread(table_lhs[...], hots)

    def place_weight(weight, slot, column):
        high, low = split(jnp.transpose(pad[slot]))
        where = slice(column * LANES, (column + 1) * LANES)
        weight[0:LANES, where] = high
        weight[LANES : 2 * LANES, where] = high
        weight[2 * LANES : 3 * LANES, where] = low

    depth = 3 * 4 * HALF
    for d in range(3):
        pad[d, 0:nb, 0:nb] = ck_ref[d]
        place_weight(w_ck, d, d)
    for i in range(4):
        pad[10 + i, 0:nf, 0:nb] = proj_ref[:, i]
        pad[10 + i, THIRD : THIRD + nf, 0:nb] = proj_ref[:, i]
        pad[10 + i, 2 * THIRD : 2 * THIRD + nf, 0:nb] = proj_ref[:, i]
        place_weight(w_proj, 10 + i, i)

    def later_weights():
        for d in range(3):
            pad[3 + d, 0:nb, 0:nb] = vol_ref[d]
            place_weight(w_own, 3 + d, d)
        pad[6:10] = jnp.zeros((4, LANES, LANES), f32)
        for i in range(4):
            pad[6 + i, 0:nf, 0:nb] = lift_ref[:, i]
        lifts = jnp.concatenate([pad[6 + i, 0:nf, :] for i in range(4)], axis=1)
        for h in range(3):
            turned = jnp.dot(
                jnp.transpose(turn_ref[h]), lifts, precision=highest, preferred_element_type=f32
            )
            for i in range(4):
                pad[14 + h * 4 + i, 0:nf, :] = turned[:, i * LANES : (i + 1) * LANES]
                high, low = split(pad[14 + h * 4 + i, 0:HALF, :])
                start = (h * 4 + i) * HALF
                w_lift[start : start + HALF, :] = high
                w_lift[depth + start : depth + start + HALF, :] = high
                w_lift[2 * depth + start : 2 * depth + start + HALF, :] = low
        for i in range(4):
            product = jnp.dot(
                jnp.transpose(proj_ref[:, i]), lifts[:, i * LANES : (i + 1) * LANES],
                precision=highest, preferred_element_type=f32,
            )
            pad[26 + i, 0:nb, :] = product
            high, low = split(pad[26 + i])
            where = slice((3 + i) * LANES, (4 + i) * LANES)
            w_own[0:LANES, where] = high
            w_own[LANES : 2 * LANES, where] = high
            w_own[2 * LANES : 3 * LANES, where] = low

    lines_misc[0:1, 0:ne] = cluster_ref[...].astype(f32)
    cluster = jnp.transpose(lines_misc[0:8])[0:ne].astype(jnp.int32)
    cluster = jnp.broadcast_to(cluster[:, 0:1], (ne, LANES))
    lengths = jnp.where(cluster == 0, 4, jnp.where(cluster == 1, 2, 1))

    def fill_choices():
        source = source_ref[...]
        is_local = source < ne
        lines_misc[8:12, 0:ne] = orient_ref[...].astype(f32)
        lines_misc[16:20, 0:ne] = jnp.where(is_local, face_ref[...] * ne + source, 1000).astype(f32)
        misc = jnp.transpose(lines_misc[...])[0:ne].astype(jnp.int32)

        def column(c):
            return jnp.broadcast_to(misc[:, c : c + 1], (ne, LANES))

        turns = [
            jnp.where(left, column(8 + 2 * side), column(9 + 2 * side)) for side in range(2)
        ]
        turn_wide = jnp.concatenate(turns, axis=1)
        for i in range(4):
            hot = jnp.where(lane_mod == column(16 + i), 1.0, 0.0)
            take_loc[i * ne : (i + 1) * ne, :] = hot.astype(bf16)
        for h in range(3):
            turn_mask[h] = jnp.where(turn_wide == h, 1.0, 0.0).astype(bf16)

    for d in range(6):
        for k in range(slots):
            send_row[d * slots + k] = faces_ref[k, d] * rows + elements_ref[k, d]

    def fill_take():
        for i in range(4):
            for e in range(ne):
                place = source_scalar[i, e] - ne
                take_row[i * ne + e] = jnp.where(place < 0, 6 * slots, place)

    for q in range(nq):
        val[q * ne : (q + 1) * ne, 0:nb] = state_ref[q]

    greeted = 4 + has_prev.astype(jnp.int32) + has_next.astype(jnp.int32)

    lane4 = lax.broadcasted_iota(jnp.int32, (4, LANES), 1)

    def copy_of(s, place):
        return pltpu.make_async_remote_copy(
            src_ref=sbuf.at[s, pl.ds(place * slots, slots)],
            dst_ref=rbuf.at[s, pl.ds(place * slots, slots)],
            send_sem=send_sem.at[s, place],
            recv_sem=recv_sem.at[s, place],
            device_id=targets[place],
            device_id_type=MESH,
        )

    def apply(x_ref, table, matrices, first, total):
        for d in range(matrices):
            for q in range(nq):
                lanes = slice((first + d) * LANES, (first + d + 1) * LANES)
                term = table[q * matrices + d].reshape(nq, ne, LANES) * x_ref[q * ne : (q + 1) * ne, lanes][None]
                total = term if total is None else total + term
        return total

    def substep(s, carry):
        phase = s & (lengths - 1)
        ending = phase + 1 == lengths
        factorial = 1.0
        groups = [slice(start, start + 8) for start in range(0, ne, 8)]
        whole = val[...].reshape(nq, ne, LANES)
        derivs = [whole[:, group] for group in groups]
        for order in range(ORDER):
            factorial = factorial * (order + 1)
            coeffs = [
                np.float32((((w + 1) * 0.25) ** (order + 1) - (w * 0.25) ** (order + 1)) / factorial)
                for w in range(4)
            ]
            w_now = jnp.where(
                phase == 0,
                coeffs[0],
                jnp.where(phase == 1, coeffs[1], jnp.where(phase == 2, coeffs[2], coeffs[3])),
            )
            for group, deriv in zip(groups, derivs):
                series[order, :, group, :] = deriv
                if order == 0:
                    cur_ref[:, group, :] = w_now[group][None] * deriv
                else:
                    cur_ref[:, group, :] += w_now[group][None] * deriv
            if order + 1 < ORDER:
                for g, deriv in enumerate(derivs):
                    halfx[g] = dot(three(deriv.reshape(nq * 8, LANES)), w_ck[...])
                derivs = []
                for g, group in enumerate(groups):
                    total = None
                    for d in range(3):
                        lanes = slice(d * LANES, (d + 1) * LANES)
                        for q in range(nq):
                            table = star_table[q * 3 + d].reshape(nq, ne, LANES)[:, group]
                            term = table * halfx[g, q * 8 : (q + 1) * 8, lanes][None]
                            total = term if total is None else total + term
                    derivs.append(total)

        for g, group in enumerate(groups):
            faces = dot(three(cur_ref[:, group, :].reshape(nq * 8, LANES)), w_proj[...])
            for j in range(4):
                for q in range(nq):
                    first = j * rows + q * ne + g * 8
                    face_rows[first : first + 8] = faces[q * 8 : (q + 1) * 8, j * LANES : (j + 1) * LANES]
        for slot in range(6 * slots):
            start = send_row[slot]
            parts = [face_rows[pl.ds(start + g * ne, 4, stride=3 * ne)] for g in range(3)]
            sbuf[s, slot] = jnp.where(
                lane4 < THIRD, parts[0], jnp.where(lane4 < 2 * THIRD, parts[1], parts[2])
            )

        @pl.when(s == 0)
        def _():
            pl.semaphore_wait(barrier, greeted)

        for place in (0, 1, 4, 5, 2, 3):
            guarded(sends[place], lambda place=place: copy_of(s, place).start())

        @pl.when(s == 0)
        def _():
            later_weights()
            fill_flux()
            fill_choices()
            fill_take()

        side_by_side = jnp.concatenate(
            [
                jnp.concatenate(
                    [face_rows[j * rows + q * ne : j * rows + (q + 1) * ne] for j in range(4)],
                    axis=0,
                )
                for q in range(nq)
            ],
            axis=1,
        )
        stacked = jnp.concatenate(split(side_by_side), axis=0)
        near = dot(take_loc[...], stacked)
        for q in range(nq):
            where = slice(q * LANES, (q + 1) * LANES)
            for side in range(2):
                acc_ref[q, :, side * LANES : (side + 1) * LANES] += jnp.where(
                    left,
                    near[2 * side * ne : (2 * side + 1) * ne, where],
                    pltpu.roll(near[(2 * side + 1) * ne : (2 * side + 2) * ne, where], HALF, 1),
                )
        own = None
        factorial = 1.0
        for order in range(ORDER):
            factorial = factorial * (order + 1)
            w_full = jnp.where(
                cluster == 0,
                np.float32(1.0 / factorial),
                jnp.where(
                    cluster == 1,
                    np.float32(0.5 ** (order + 1) / factorial),
                    np.float32(0.25 ** (order + 1) / factorial),
                ),
            )
            term = w_full[None] * series[order]
            own = term if own is None else own + term
        xs[...] = dot(three(own.reshape(rows, LANES)), w_own[...])
        loc_ref[...] = apply(xs, local_table, 4, 3, apply(xs, star_table, 3, 0, None))

        for place in range(6):
            guarded(arrives[place], lambda place=place: copy_of(s, place).wait_recv())
        arrived[0 : 6 * slots] = rbuf[s]
        for row in range(4 * ne):
            got_rows[pl.ds(row, 4, stride=4 * ne)] = arrived[take_row[row]]

        def got(t, i):
            return got_rows[(t * 4 + i) * ne : (t * 4 + i + 1) * ne]

        ending_wide = jnp.concatenate([ending, ending], axis=1)
        total = None
        for q in range(nq):
            t, g = divmod(q, 3)
            sides = []
            for side in range(2):
                first, second = got(t, 2 * side), got(t, 2 * side + 1)
                if g:
                    first = pltpu.roll(first, LANES - g * THIRD, 1)
                second = pltpu.roll(second, (HALF - g * THIRD) % LANES, 1)
                sides.append(jnp.where(left, first, second))
            wide = acc_ref[q] + jnp.concatenate(sides, axis=1)
            term = far_table[q].reshape(nq, ne, 2 * LANES) * wide[None]
            total = term if total is None else total + term
            acc_ref[q] = jnp.where(ending_wide, 0.0, wide)
        parts = [part.reshape(nq, ne, 2 * LANES) for part in split(total.reshape(rows, 2 * LANES))]
        high, low = [
            [(part * turn_mask[h][None]).reshape(rows, 2 * LANES) for h in range(3)] for part in parts
        ]
        masked = jnp.concatenate(high + low + high, axis=1)
        upd = dot(masked, w_lift[...]).reshape(nq, ne, LANES) + loc_ref[...]
        old = val[...].reshape(nq, ne, LANES)
        val[...] = jnp.where(ending[None], old + upd, old).reshape(rows, LANES)
        return carry

    lax.fori_loop(0, SUBSTEPS, substep, 0)
    out_ref[...] = val[...].reshape(nq, ne, LANES)

    def drain(s, carry):
        for place in range(6):
            guarded(sends[place], lambda place=place: copy_of(s, place).wait_send())
        return carry

    lax.fori_loop(0, SUBSTEPS, drain, 0)


def shards(
    n_dom, n_sub,
    state, ck_matrices, vol_matrices, face_project, face_lift, face_turn,
    star_matrices, flux_local, flux_neighbor, cluster,
    send_elements, send_faces, neighbor_source, neighbor_face, neighbor_turn,
):
    nq, nb, ne = state.shape
    nf = face_project.shape[1]
    rows = nq * ne
    slots = send_elements.shape[3]
    operands = [
        state.transpose(0, 2, 1),
        ck_matrices,
        vol_matrices,
        face_project.transpose(1, 0, 2),
        face_lift.transpose(2, 0, 1),
        face_turn,
        star_matrices.transpose(1, 2, 0, 3),
        flux_local.transpose(1, 2, 0, 3),
        flux_neighbor.transpose(1, 2, 0, 3),
        cluster[None],
        send_elements[0, 0].T,
        send_faces[0, 0].T,
        neighbor_source,
        neighbor_face,
        neighbor_turn,
    ]
    whole = pl.BlockSpec(memory_space=pltpu.VMEM)
    result = pl.pallas_call(
        functools.partial(kernel, n_dom, n_sub, nq, ne, nb, nf),
        out_shape=pltpu.VMEM((nq, ne, LANES), f32),
        in_specs=[pl.BlockSpec(memory_space=pltpu.HBM)] * len(operands),
        out_specs=whole,
        scratch_shapes=[
            *[(pltpu.SMEM if k in (10, 11) else pltpu.VMEM)(x.shape, x.dtype) for k, x in enumerate(operands)],
            pltpu.SMEM(neighbor_source.shape, jnp.int32),
            pltpu.SemaphoreType.DMA((len(operands) + 1,)),
            pltpu.VMEM((30, LANES, LANES), f32),
            pltpu.VMEM((nq, 32, LANES), f32),
            pltpu.VMEM((nq, 8 * nq, LANES), f32),
            pltpu.VMEM((nq, ne, 8 * nq), f32),
            pltpu.VMEM((32, LANES), f32),
            pltpu.VMEM((3 * LANES, 3 * LANES), bf16),
            pltpu.VMEM((3 * LANES, 7 * LANES), bf16),
            pltpu.VMEM((3 * LANES, 4 * LANES), bf16),
            pltpu.VMEM((3 * 3 * 4 * HALF, LANES), bf16),
            pltpu.VMEM((2 * rows, 8 * nq), bf16),
            pltpu.VMEM((3 * nq + 1, rows, LANES), f32),
            pltpu.VMEM((4 * nq, rows, LANES), f32),
            pltpu.VMEM((nq, rows, 2 * LANES), f32),
            pltpu.VMEM((rows, LANES), f32),
            pltpu.VMEM((rows, 7 * LANES), f32),
            pltpu.VMEM((ne // 8, nq * 8, 3 * LANES), f32),
            pltpu.VMEM((ORDER, nq, ne, LANES), f32),
            pltpu.VMEM((nq, ne, LANES), f32),
            pltpu.VMEM((nq, ne, LANES), f32),
            pltpu.VMEM((nq, ne, 2 * LANES), f32),
            pltpu.VMEM((4 * ne, LANES), bf16),
            pltpu.VMEM((3, ne, 2 * LANES), bf16),
            pltpu.VMEM((4 * rows + 16 * ne, LANES), f32),
            pltpu.VMEM((4 * 4 * ne, LANES), f32),
            pltpu.SMEM((6 * slots,), jnp.int32),
            pltpu.SMEM((4 * ne,), jnp.int32),
            pltpu.VMEM((SUBSTEPS, 6 * slots, 4, LANES), f32),
            pltpu.VMEM((SUBSTEPS, 6 * slots, 4, LANES), f32),
            pltpu.VMEM((6 * slots + 1, 4, LANES), f32),
            pltpu.SemaphoreType.DMA((SUBSTEPS, 6)),
            pltpu.SemaphoreType.DMA((SUBSTEPS, 6)),
        ],
        compiler_params=pltpu.CompilerParams(
            collective_id=0, has_side_effects=True, vmem_limit_bytes=24 * 1024 * 1024
        ),
    )(*[pltpu.with_memory_space_constraint(x, pltpu.HBM) for x in operands])
    return result[:, :, 0:nb].transpose(0, 2, 1)


def solution(mesh):
    both = ("dom", "sub")
    in_specs = (
        P(None, None, both),
        P(),
        P(),
        P(),
        P(),
        P(),
        P(None, None, None, both),
        P(None, None, None, both),
        P(None, None, None, both),
        P(both),
        P("dom", "sub", None, None),
        P("dom", "sub", None, None),
        P(None, both),
        P(None, both),
        P(None, both),
    )
    return jax.shard_map(
        functools.partial(shards, mesh.shape["dom"], mesh.shape["sub"]),
        mesh=mesh,
        in_specs=in_specs,
        out_specs=P(None, None, both),
        check_vma=False,
    )
```

```python
import functools
import math

import jax
import jax.numpy as jnp
import numpy as np
from jax import lax
from jax.experimental import pallas as pl
from jax.experimental.pallas import tpu as pltpu
from jax.sharding import PartitionSpec as P

ORDER = 8
SUBSTEPS = 4
LANES = 128
HALF = 64
THIRD = 40

MESH = pl.DeviceIdType.MESH
f32 = jnp.float32
bf16 = jnp.bfloat16
highest = lax.Precision.HIGHEST


def split(x):
    high = x.astype(bf16)
    low = (x - high.astype(f32)).astype(bf16)
    return high, low


def three(x):
    high, low = split(x)
    return jnp.concatenate([high, low, high], axis=1)


def dot(a, b):
    return jnp.dot(a, b, preferred_element_type=f32)


def kernel(
    n_dom, n_sub, nq, ne, nb, nf,
    state_hbm, ck_hbm, vol_hbm, proj_hbm, lift_hbm, turn_hbm, star_hbm, local_hbm, far_hbm,
    cluster_hbm, elements_hbm, faces_hbm, source_hbm, face_hbm, orient_hbm,
    out_ref,
    state_ref, ck_ref, vol_ref, proj_ref, lift_ref, turn_ref, star_ref, local_ref, far_ref,
    cluster_ref, elements_ref, faces_ref, source_ref, face_ref, orient_ref, source_scalar, in_sem,
    pad, star_lines, lines, columns, lines_misc, w_ck, w_own, w_proj, w_lift,
    table_lhs, star_table, local_table, far_table,
    val, xs, halfx, series, cur_ref, loc_ref, acc_ref, take_loc, turn_mask, face_rows, got_rows,
    send_row, take_row, sbuf, rbuf, arrived, send_sem, recv_sem,
):
    rows = nq * ne
    slots = elements_ref.shape[0]
    dom = lax.axis_index("dom")
    sub = lax.axis_index("sub")
    has_prev = dom > 0
    has_next = dom < n_dom - 1
    targets = [
        (dom + 1, sub),
        (dom - 1, sub),
        (dom, lax.rem(sub + 1, n_sub)),
        (dom, lax.rem(sub + n_sub - 1, n_sub)),
        (dom, lax.rem(sub + 2, n_sub)),
        (dom, lax.rem(sub + n_sub - 2, n_sub)),
    ]
    sends = [has_next, has_prev, None, None, None, None]
    arrives = [has_prev, has_next, None, None, None, None]

    barrier = pltpu.get_barrier_semaphore()

    def guarded(flag, action):
        if flag is None:
            action()
        else:
            pl.when(flag)(action)

    for place in range(6):
        guarded(
            sends[place],
            lambda place=place: pl.semaphore_signal(
                barrier, inc=1, device_id=targets[place], device_id_type=MESH
            ),
        )

    from_refs = [
        star_hbm, ck_hbm, state_hbm, local_hbm, far_hbm, cluster_hbm, elements_hbm, faces_hbm,
        source_hbm, face_hbm, orient_hbm, proj_hbm, lift_hbm, turn_hbm, vol_hbm, source_hbm,
    ]
    to_refs = [
        star_ref, ck_ref, state_ref, local_ref, far_ref, cluster_ref, elements_ref, faces_ref,
        source_ref, face_ref, orient_ref, proj_ref, lift_ref, turn_ref, vol_ref, source_scalar,
    ]
    loads = [
        pltpu.make_async_copy(from_refs[k], to_refs[k], in_sem.at[k]) for k in range(len(to_refs))
    ]
    for load in loads:
        load.start()

    lane = lax.broadcasted_iota(jnp.int32, (ne, LANES), 1)
    left = lane < HALF
    lane_mod = lane & (HALF - 1)

    @pl.when(dom == 0)
    def _():
        rbuf[:, 0:slots] = jnp.zeros((SUBSTEPS, slots, 4, LANES), f32)

    @pl.when(dom == n_dom - 1)
    def _():
        rbuf[:, slots : 2 * slots] = jnp.zeros((SUBSTEPS, slots, 4, LANES), f32)

    pad[...] = jnp.zeros_like(pad)
    star_lines[...] = jnp.zeros_like(star_lines)
    lines_misc[...] = jnp.zeros_like(lines_misc)
    val[...] = jnp.zeros_like(val)
    acc_ref[...] = jnp.zeros_like(acc_ref)
    face_rows[4 * rows :] = jnp.zeros((face_rows.shape[0] - 4 * rows, LANES), f32)
    arrived[6 * slots] = jnp.zeros((4, LANES), f32)
    for load in loads:
        load.wait()

    for p in range(nq):
        for q in range(nq):
            star_lines[p, q * 3 : q * 3 + 3, 0:ne] = star_ref[p, q]
    star_columns = [jnp.transpose(star_lines[p])[0:ne] for p in range(nq)]
    star_lhs = jnp.concatenate(split(jnp.concatenate(star_columns, axis=0)), axis=0)
    pick = lax.broadcasted_iota(jnp.int32, (LANES, LANES), 0)
    left_pick = lax.broadcasted_iota(jnp.int32, (LANES, LANES), 1) < HALF

    def spread(lhs, hots):
        both = dot(lhs, jnp.concatenate(hots, axis=1))
        return both[0:rows] + both[rows : 2 * rows]

    def one_hot(j, depth):
        return jnp.where(pick[0:depth] == j, 1.0, 0.0).astype(bf16)

    for j in range(0, 3 * nq, 2):
        pair = spread(star_lhs, [one_hot(j, 32), one_hot(j + 1, 32)])
        star_table[j] = pair[:, 0:LANES]
        star_table[j + 1] = pair[:, LANES : 2 * LANES]

    def fill_flux():
        lines[...] = jnp.zeros_like(lines)
        for p in range(nq):
            for q in range(nq):
                lines[p, q * 4 : q * 4 + 4, 0:ne] = -local_ref[p, q]
                lines[p, 4 * nq + q * 4 : 4 * nq + q * 4 + 4, 0:ne] = -far_ref[p, q]
        for p in range(nq):
            columns[p] = jnp.transpose(lines[p])[0:ne]
        table_lhs[...] = jnp.concatenate(split(columns[...].reshape(rows, 8 * nq)), axis=0)
        for j in range(0, 4 * nq, 2):
            pair = spread(table_lhs[...], [one_hot(j, 8 * nq), one_hot(j + 1, 8 * nq)])
            local_table[j] = pair[:, 0:LANES]
            local_table[j + 1] = pair[:, LANES : 2 * LANES]
        for q in range(nq):
            hots = []
            for side in range(2):
                j = 4 * nq + q * 4 + 2 * side
                hots.append(
                    jnp.where(pick[0 : 8 * nq] == jnp.where(left_pick[0 : 8 * nq], j, j + 1), 1.0, 0.0).astype(bf16)
                )
            far_table[q] = spread(table_lhs[...], hots)

    def place_weight(weight, slot, column):
        high, low = split(jnp.transpose(pad[slot]))
        where = slice(column * LANES, (column + 1) * LANES)
        weight[0:LANES, where] = high
        weight[LANES : 2 * LANES, where] = high
        weight[2 * LANES : 3 * LANES, where] = low

    for d in range(3):
        pad[d, 0:nb, 0:nb] = ck_ref[d]
        place_weight(w_ck, d, d)
    for i in range(4):
        pad[10 + i, 0:nf, 0:nb] = proj_ref[:, i]
        pad[10 + i, THIRD : THIRD + nf, 0:nb] = proj_ref[:, i]
        pad[10 + i, 2 * THIRD : 2 * THIRD + nf, 0:nb] = proj_ref[:, i]
        place_weight(w_proj, 10 + i, i)

    def later_weights():
        for d in range(3):
            pad[3 + d, 0:nb, 0:nb] = vol_ref[d]
            place_weight(w_own, 3 + d, d)
        pad[6:10] = jnp.zeros((4, LANES, LANES), f32)
        for i in range(4):
            pad[6 + i, 0:nf, 0:nb] = lift_ref[:, i]
        lifts = jnp.concatenate([pad[6 + i, 0:nf, :] for i in range(4)], axis=1)
        for h in range(3):
            turned = jnp.dot(
                jnp.transpose(turn_ref[h]), lifts, precision=highest, preferred_element_type=f32
            )
            for i in range(4):
                pad[14 + h * 4 + i, 0:nf, :] = turned[:, i * LANES : (i + 1) * LANES]
                high, low = split(pad[14 + h * 4 + i, 0:HALF, :])
                start = (h * 4 + i) * HALF
                w_lift[start : start + HALF, 0:LANES] = high
                w_lift[start : start + HALF, LANES : 2 * LANES] = low
        for i in range(4):
            product = jnp.dot(
                jnp.transpose(proj_ref[:, i]), lifts[:, i * LANES : (i + 1) * LANES],
                precision=highest, preferred_element_type=f32,
            )
            pad[26 + i, 0:nb, :] = product
            high, low = split(pad[26 + i])
            where = slice((3 + i) * LANES, (4 + i) * LANES)
            w_own[0:LANES, where] = high
            w_own[LANES : 2 * LANES, where] = high
            w_own[2 * LANES : 3 * LANES, where] = low

    lines_misc[0:1, 0:ne] = cluster_ref[...].astype(f32)
    cluster = jnp.transpose(lines_misc[0:8])[0:ne].astype(jnp.int32)
    cluster = jnp.broadcast_to(cluster[:, 0:1], (ne, LANES))
    lengths = jnp.where(cluster == 0, 4, jnp.where(cluster == 1, 2, 1))

    def fill_choices():
        source = source_ref[...]
        is_local = source < ne
        lines_misc[8:12, 0:ne] = orient_ref[...].astype(f32)
        lines_misc[16:20, 0:ne] = jnp.where(is_local, face_ref[...] * ne + source, 1000).astype(f32)
        misc = jnp.transpose(lines_misc[...])[0:ne].astype(jnp.int32)

        def column(c):
            return jnp.broadcast_to(misc[:, c : c + 1], (ne, LANES))

        turns = [
            jnp.where(left, column(8 + 2 * side), column(9 + 2 * side)) for side in range(2)
        ]
        turn_wide = jnp.concatenate(turns, axis=1)
        for i in range(4):
            hot = jnp.where(lane_mod == column(16 + i), 1.0, 0.0)
            take_loc[i * ne : (i + 1) * ne, :] = hot.astype(bf16)
        for h in range(3):
            turn_mask[h] = jnp.where(turn_wide == h, 1.0, 0.0).astype(bf16)

    for d in range(6):
        for k in range(slots):
            send_row[d * slots + k] = faces_ref[k, d] * rows + elements_ref[k, d]

    def fill_take():
        for i in range(4):
            for e in range(ne):
                place = source_scalar[i, e] - ne
                take_row[i * ne + e] = jnp.where(place < 0, 6 * slots, place)

    for q in range(nq):
        val[q * ne : (q + 1) * ne, 0:nb] = state_ref[q]

    greeted = 4 + has_prev.astype(jnp.int32) + has_next.astype(jnp.int32)

    lane4 = lax.broadcasted_iota(jnp.int32, (4, LANES), 1)

    def copy_of(s, place):
        return pltpu.make_async_remote_copy(
            src_ref=sbuf.at[s, pl.ds(place * slots, slots)],
            dst_ref=rbuf.at[s, pl.ds(place * slots, slots)],
            send_sem=send_sem.at[s, place],
            recv_sem=recv_sem.at[s, place],
            device_id=targets[place],
            device_id_type=MESH,
        )

    def apply(x_ref, table, matrices, first, total):
        for d in range(matrices):
            for q in range(nq):
                lanes = slice((first + d) * LANES, (first + d + 1) * LANES)
                term = table[q * matrices + d].reshape(nq, ne, LANES) * x_ref[q * ne : (q + 1) * ne, lanes][None]
                total = term if total is None else total + term
        return total

    def substep(s, carry):
        phase = s & (lengths - 1)
        ending = phase + 1 == lengths
        factorial = 1.0
        groups = [slice(start, start + 8) for start in range(0, ne, 8)]
        whole = val[...].reshape(nq, ne, LANES)
        derivs = [whole[:, group] for group in groups]
        for order in range(ORDER):
            factorial = factorial * (order + 1)
            coeffs = [
                np.float32((((w + 1) * 0.25) ** (order + 1) - (w * 0.25) ** (order + 1)) / factorial)
                for w in range(4)
            ]
            w_now = jnp.where(
                phase == 0,
                coeffs[0],
                jnp.where(phase == 1, coeffs[1], jnp.where(phase == 2, coeffs[2], coeffs[3])),
            )
            for group, deriv in zip(groups, derivs):
                series[order, :, group, :] = deriv
                if order == 0:
                    cur_ref[:, group, :] = w_now[group][None] * deriv
                else:
                    cur_ref[:, group, :] += w_now[group][None] * deriv
            if order + 1 < ORDER:
                for g, deriv in enumerate(derivs):
                    halfx[g] = dot(three(deriv.reshape(nq * 8, LANES)), w_ck[...])
                derivs = []
                for g, group in enumerate(groups):
                    total = None
                    for d in range(3):
                        lanes = slice(d * LANES, (d + 1) * LANES)
                        for q in range(nq):
                            table = star_table[q * 3 + d].reshape(nq, ne, LANES)[:, group]
                            term = table * halfx[g, q * 8 : (q + 1) * 8, lanes][None]
                            total = term if total is None else total + term
                    derivs.append(total)

        for g, group in enumerate(groups):
            faces = dot(three(cur_ref[:, group, :].reshape(nq * 8, LANES)), w_proj[...])
            for j in range(4):
                for q in range(nq):
                    first = j * rows + q * ne + g * 8
                    face_rows[first : first + 8] = faces[q * 8 : (q + 1) * 8, j * LANES : (j + 1) * LANES]
        @pl.when(s == 0)
        def _():
            pl.semaphore_wait(barrier, greeted)

        for place in (0, 1, 4, 5, 2, 3):
            for slot in range(place * slots, (place + 1) * slots):
                start = send_row[slot]
                parts = [face_rows[pl.ds(start + g * ne, 4, stride=3 * ne)] for g in range(3)]
                sbuf[s, slot] = jnp.where(
                    lane4 < THIRD, parts[0], jnp.where(lane4 < 2 * THIRD, parts[1], parts[2])
                )
            guarded(sends[place], lambda place=place: copy_of(s, place).start())

        @pl.when(s == 0)
        def _():
            later_weights()
            fill_flux()
            fill_choices()
            fill_take()

        side_by_side = jnp.concatenate(
            [
                jnp.concatenate(
                    [face_rows[j * rows + q * ne : j * rows + (q + 1) * ne] for j in range(4)],
                    axis=0,
                )
                for q in range(nq)
            ],
            axis=1,
        )
        stacked = jnp.concatenate(split(side_by_side), axis=0)
        near = dot(take_loc[...], stacked)
        for q in range(nq):
            where = slice(q * LANES, (q + 1) * LANES)
            for side in range(2):
                acc_ref[q, :, side * LANES : (side + 1) * LANES] += jnp.where(
                    left,
                    near[2 * side * ne : (2 * side + 1) * ne, where],
                    pltpu.roll(near[(2 * side + 1) * ne : (2 * side + 2) * ne, where], HALF, 1),
                )
        own = None
        factorial = 1.0
        for order in range(ORDER):
            factorial = factorial * (order + 1)
            w_full = jnp.where(
                cluster == 0,
                np.float32(1.0 / factorial),
                jnp.where(
                    cluster == 1,
                    np.float32(0.5 ** (order + 1) / factorial),
                    np.float32(0.25 ** (order + 1) / factorial),
                ),
            )
            term = w_full[None] * series[order]
            own = term if own is None else own + term
        xs[...] = dot(three(own.reshape(rows, LANES)), w_own[...])
        loc_ref[...] = apply(xs, local_table, 4, 3, apply(xs, star_table, 3, 0, None))

        for place in range(6):
            guarded(arrives[place], lambda place=place: copy_of(s, place).wait_recv())
        arrived[0 : 6 * slots] = rbuf[s]
        for row in range(4 * ne):
            got_rows[pl.ds(row, 4, stride=4 * ne)] = arrived[take_row[row]]

        def got(t, i):
            return got_rows[(t * 4 + i) * ne : (t * 4 + i + 1) * ne]

        ending_wide = jnp.concatenate([ending, ending], axis=1)
        total = None
        for q in range(nq):
            t, g = divmod(q, 3)
            sides = []
            for side in range(2):
                first, second = got(t, 2 * side), got(t, 2 * side + 1)
                if g:
                    first = pltpu.roll(first, LANES - g * THIRD, 1)
                second = pltpu.roll(second, (HALF - g * THIRD) % LANES, 1)
                sides.append(jnp.where(left, first, second))
            wide = acc_ref[q] + jnp.concatenate(sides, axis=1)
            term = far_table[q].reshape(nq, ne, 2 * LANES) * wide[None]
            total = term if total is None else total + term
            acc_ref[q] = jnp.where(ending_wide, 0.0, wide)
        parts = [part.reshape(nq, ne, 2 * LANES) for part in split(total.reshape(rows, 2 * LANES))]
        high, low = [
            [(part * turn_mask[h][None]).reshape(rows, 2 * LANES) for h in range(3)] for part in parts
        ]
        masked = jnp.concatenate(
            [jnp.concatenate(high, axis=1), jnp.concatenate(low, axis=1)], axis=0
        )
        both = dot(masked, w_lift[...])
        upd = both[0:rows, 0:LANES] + both[0:rows, LANES : 2 * LANES] + both[rows:, 0:LANES]
        upd = upd.reshape(nq, ne, LANES) + loc_ref[...]
        old = val[...].reshape(nq, ne, LANES)
        val[...] = jnp.where(ending[None], old + upd, old).reshape(rows, LANES)
        return carry

    lax.fori_loop(0, SUBSTEPS, substep, 0)
    out_ref[...] = val[...].reshape(nq, ne, LANES)

    def drain(s, carry):
        for place in range(6):
            guarded(sends[place], lambda place=place: copy_of(s, place).wait_send())
        return carry

    lax.fori_loop(0, SUBSTEPS, drain, 0)


def shards(
    n_dom, n_sub,
    state, ck_matrices, vol_matrices, face_project, face_lift, face_turn,
    star_matrices, flux_local, flux_neighbor, cluster,
    send_elements, send_faces, neighbor_source, neighbor_face, neighbor_turn,
):
    nq, nb, ne = state.shape
    nf = face_project.shape[1]
    rows = nq * ne
    slots = send_elements.shape[3]
    operands = [
        state.transpose(0, 2, 1),
        ck_matrices,
        vol_matrices,
        face_project.transpose(1, 0, 2),
        face_lift.transpose(2, 0, 1),
        face_turn,
        star_matrices.transpose(1, 2, 0, 3),
        flux_local.transpose(1, 2, 0, 3),
        flux_neighbor.transpose(1, 2, 0, 3),
        cluster[None],
        send_elements[0, 0].T,
        send_faces[0, 0].T,
        neighbor_source,
        neighbor_face,
        neighbor_turn,
    ]
    whole = pl.BlockSpec(memory_space=pltpu.VMEM)
    result = pl.pallas_call(
        functools.partial(kernel, n_dom, n_sub, nq, ne, nb, nf),
        out_shape=pltpu.VMEM((nq, ne, LANES), f32),
        in_specs=[pl.BlockSpec(memory_space=pltpu.HBM)] * len(operands),
        out_specs=whole,
        scratch_shapes=[
            *[(pltpu.SMEM if k in (10, 11) else pltpu.VMEM)(x.shape, x.dtype) for k, x in enumerate(operands)],
            pltpu.SMEM(neighbor_source.shape, jnp.int32),
            pltpu.SemaphoreType.DMA((len(operands) + 1,)),
            pltpu.VMEM((30, LANES, LANES), f32),
            pltpu.VMEM((nq, 32, LANES), f32),
            pltpu.VMEM((nq, 8 * nq, LANES), f32),
            pltpu.VMEM((nq, ne, 8 * nq), f32),
            pltpu.VMEM((32, LANES), f32),
            pltpu.VMEM((3 * LANES, 3 * LANES), bf16),
            pltpu.VMEM((3 * LANES, 7 * LANES), bf16),
            pltpu.VMEM((3 * LANES, 4 * LANES), bf16),
            pltpu.VMEM((3 * 4 * HALF, 2 * LANES), bf16),
            pltpu.VMEM((2 * rows, 8 * nq), bf16),
            pltpu.VMEM((3 * nq + 1, rows, LANES), f32),
            pltpu.VMEM((4 * nq, rows, LANES), f32),
            pltpu.VMEM((nq, rows, 2 * LANES), f32),
            pltpu.VMEM((rows, LANES), f32),
            pltpu.VMEM((rows, 7 * LANES), f32),
            pltpu.VMEM((ne // 8, nq * 8, 3 * LANES), f32),
            pltpu.VMEM((ORDER, nq, ne, LANES), f32),
            pltpu.VMEM((nq, ne, LANES), f32),
            pltpu.VMEM((nq, ne, LANES), f32),
            pltpu.VMEM((nq, ne, 2 * LANES), f32),
            pltpu.VMEM((4 * ne, LANES), bf16),
            pltpu.VMEM((3, ne, 2 * LANES), bf16),
            pltpu.VMEM((4 * rows + 16 * ne, LANES), f32),
            pltpu.VMEM((4 * 4 * ne, LANES), f32),
            pltpu.SMEM((6 * slots,), jnp.int32),
            pltpu.SMEM((4 * ne,), jnp.int32),
            pltpu.VMEM((SUBSTEPS, 6 * slots, 4, LANES), f32),
            pltpu.VMEM((SUBSTEPS, 6 * slots, 4, LANES), f32),
            pltpu.VMEM((6 * slots + 1, 4, LANES), f32),
            pltpu.SemaphoreType.DMA((SUBSTEPS, 6)),
            pltpu.SemaphoreType.DMA((SUBSTEPS, 6)),
        ],
        compiler_params=pltpu.CompilerParams(
            collective_id=0, has_side_effects=True, vmem_limit_bytes=24 * 1024 * 1024
        ),
    )(*[pltpu.with_memory_space_constraint(x, pltpu.HBM) for x in operands])
    return result[:, :, 0:nb].transpose(0, 2, 1)


def solution(mesh):
    both = ("dom", "sub")
    in_specs = (
        P(None, None, both),
        P(),
        P(),
        P(),
        P(),
        P(),
        P(None, None, None, both),
        P(None, None, None, both),
        P(None, None, None, both),
        P(both),
        P("dom", "sub", None, None),
        P("dom", "sub", None, None),
        P(None, both),
        P(None, both),
        P(None, both),
    )
    return jax.shard_map(
        functools.partial(shards, mesh.shape["dom"], mesh.shape["sub"]),
        mesh=mesh,
        in_specs=in_specs,
        out_specs=P(None, None, both),
        check_vma=False,
    )
```

```python
import functools
import math

import jax
import jax.numpy as jnp
import numpy as np
from jax import lax
from jax.experimental import pallas as pl
from jax.experimental.pallas import tpu as pltpu
from jax.sharding import PartitionSpec as P

ORDER = 8
SUBSTEPS = 4
LANES = 128
HALF = 64
THIRD = 40

MESH = pl.DeviceIdType.MESH
f32 = jnp.float32
bf16 = jnp.bfloat16
highest = lax.Precision.HIGHEST


def split(x):
    high = x.astype(bf16)
    low = (x - high.astype(f32)).astype(bf16)
    return high, low


def three(x):
    high, low = split(x)
    return jnp.concatenate([high, low, high], axis=1)


def dot(a, b):
    return jnp.dot(a, b, preferred_element_type=f32)


def kernel(
    n_dom, n_sub, nq, ne, nb, nf,
    state_hbm, ck_hbm, vol_hbm, proj_hbm, lift_hbm, turn_hbm, star_hbm, local_hbm, far_hbm,
    cluster_hbm, elements_hbm, faces_hbm, source_hbm, face_hbm, orient_hbm,
    out_ref,
    state_ref, ck_ref, vol_ref, proj_ref, lift_ref, turn_ref, star_ref, local_ref, far_ref,
    cluster_ref, elements_ref, faces_ref, source_ref, face_ref, orient_ref, source_scalar, in_sem,
    pad, star_lines, lines, columns, lines_misc, w_ck, w_own, w_proj, w_lift,
    table_lhs, star_table, local_table, far_table,
    val, xs, halfx, series, cur_ref, loc_ref, acc_ref, take_loc, turn_mask, face_rows, got_rows,
    send_row, take_row, sbuf, rbuf, arrived, send_sem, recv_sem,
):
    rows = nq * ne
    slots = elements_ref.shape[0]
    dom = lax.axis_index("dom")
    sub = lax.axis_index("sub")
    has_prev = dom > 0
    has_next = dom < n_dom - 1
    targets = [
        (dom + 1, sub),
        (dom - 1, sub),
        (dom, lax.rem(sub + 1, n_sub)),
        (dom, lax.rem(sub + n_sub - 1, n_sub)),
        (dom, lax.rem(sub + 2, n_sub)),
        (dom, lax.rem(sub + n_sub - 2, n_sub)),
    ]
    sends = [has_next, has_prev, None, None, None, None]
    arrives = [has_prev, has_next, None, None, None, None]

    barrier = pltpu.get_barrier_semaphore()

    def guarded(flag, action):
        if flag is None:
            action()
        else:
            pl.when(flag)(action)

    for place in range(6):
        guarded(
            sends[place],
            lambda place=place: pl.semaphore_signal(
                barrier, inc=1, device_id=targets[place], device_id_type=MESH
            ),
        )

    from_refs = [
        star_hbm, ck_hbm, state_hbm, local_hbm, far_hbm, cluster_hbm, elements_hbm, faces_hbm,
        source_hbm, face_hbm, orient_hbm, proj_hbm, lift_hbm, turn_hbm, vol_hbm, source_hbm,
    ]
    to_refs = [
        star_ref, ck_ref, state_ref, local_ref, far_ref, cluster_ref, elements_ref, faces_ref,
        source_ref, face_ref, orient_ref, proj_ref, lift_ref, turn_ref, vol_ref, source_scalar,
    ]
    loads = [
        pltpu.make_async_copy(from_refs[k], to_refs[k], in_sem.at[k]) for k in range(len(to_refs))
    ]
    for load in loads:
        load.start()

    lane = lax.broadcasted_iota(jnp.int32, (ne, LANES), 1)
    left = lane < HALF
    lane_mod = lane & (HALF - 1)

    pad[...] = jnp.zeros_like(pad)
    star_lines[...] = jnp.zeros_like(star_lines)
    lines_misc[...] = jnp.zeros_like(lines_misc)
    val[...] = jnp.zeros_like(val)
    acc_ref[...] = jnp.zeros_like(acc_ref)
    face_rows[4 * rows :] = jnp.zeros((face_rows.shape[0] - 4 * rows, LANES), f32)
    arrived[...] = jnp.zeros_like(arrived)
    for load in loads:
        load.wait()

    for p in range(nq):
        for q in range(nq):
            star_lines[p, q * 3 : q * 3 + 3, 0:ne] = star_ref[p, q]
    star_columns = [jnp.transpose(star_lines[p])[0:ne] for p in range(nq)]
    star_lhs = jnp.concatenate(split(jnp.concatenate(star_columns, axis=0)), axis=0)
    pick = lax.broadcasted_iota(jnp.int32, (LANES, LANES), 0)
    left_pick = lax.broadcasted_iota(jnp.int32, (LANES, LANES), 1) < HALF

    def spread(lhs, hots):
        both = dot(lhs, jnp.concatenate(hots, axis=1))
        return both[0:rows] + both[rows : 2 * rows]

    def one_hot(j, depth):
        return jnp.where(pick[0:depth] == j, 1.0, 0.0).astype(bf16)

    for j in range(0, 3 * nq, 2):
        pair = spread(star_lhs, [one_hot(j, 32), one_hot(j + 1, 32)])
        star_table[j] = pair[:, 0:LANES]
        star_table[j + 1] = pair[:, LANES : 2 * LANES]

    def fill_flux():
        lines[...] = jnp.zeros_like(lines)
        for p in range(nq):
            for q in range(nq):
                lines[p, q * 4 : q * 4 + 4, 0:ne] = -local_ref[p, q]
                lines[p, 4 * nq + q * 4 : 4 * nq + q * 4 + 4, 0:ne] = -far_ref[p, q]
        for p in range(nq):
            columns[p] = jnp.transpose(lines[p])[0:ne]
        table_lhs[...] = jnp.concatenate(split(columns[...].reshape(rows, 8 * nq)), axis=0)
        for j in range(0, 4 * nq, 2):
            pair = spread(table_lhs[...], [one_hot(j, 8 * nq), one_hot(j + 1, 8 * nq)])
            local_table[j] = pair[:, 0:LANES]
            local_table[j + 1] = pair[:, LANES : 2 * LANES]
        for q in range(nq):
            hots = []
            for side in range(2):
                j = 4 * nq + q * 4 + 2 * side
                hots.append(
                    jnp.where(pick[0 : 8 * nq] == jnp.where(left_pick[0 : 8 * nq], j, j + 1), 1.0, 0.0).astype(bf16)
                )
            far_table[q] = spread(table_lhs[...], hots)

    def place_weight(weight, slot, column):
        high, low = split(jnp.transpose(pad[slot]))
        where = slice(column * LANES, (column + 1) * LANES)
        weight[0:LANES, where] = high
        weight[LANES : 2 * LANES, where] = high
        weight[2 * LANES : 3 * LANES, where] = low

    for d in range(3):
        pad[d, 0:nb, 0:nb] = ck_ref[d]
        place_weight(w_ck, d, d)
    for i in range(4):
        pad[10 + i, 0:nf, 0:nb] = proj_ref[:, i]
        pad[10 + i, THIRD : THIRD + nf, 0:nb] = proj_ref[:, i]
        pad[10 + i, 2 * THIRD : 2 * THIRD + nf, 0:nb] = proj_ref[:, i]
        place_weight(w_proj, 10 + i, i)

    def later_weights():
        for d in range(3):
            pad[3 + d, 0:nb, 0:nb] = vol_ref[d]
            place_weight(w_own, 3 + d, d)
        pad[6:10] = jnp.zeros((4, LANES, LANES), f32)
        for i in range(4):
            pad[6 + i, 0:nf, 0:nb] = lift_ref[:, i]
        lifts = jnp.concatenate([pad[6 + i, 0:nf, :] for i in range(4)], axis=1)
        for h in range(3):
            turned = jnp.dot(
                jnp.transpose(turn_ref[h]), lifts, precision=highest, preferred_element_type=f32
            )
            for i in range(4):
                pad[14 + h * 4 + i, 0:nf, :] = turned[:, i * LANES : (i + 1) * LANES]
                high, low = split(pad[14 + h * 4 + i, 0:HALF, :])
                start = (h * 4 + i) * HALF
                w_lift[start : start + HALF, 0:LANES] = high
                w_lift[start : start + HALF, LANES : 2 * LANES] = low
        for i in range(4):
            product = jnp.dot(
                jnp.transpose(proj_ref[:, i]), lifts[:, i * LANES : (i + 1) * LANES],
                precision=highest, preferred_element_type=f32,
            )
            pad[26 + i, 0:nb, :] = product
            high, low = split(pad[26 + i])
            where = slice((3 + i) * LANES, (4 + i) * LANES)
            w_own[0:LANES, where] = high
            w_own[LANES : 2 * LANES, where] = high
            w_own[2 * LANES : 3 * LANES, where] = low

    lines_misc[0:1, 0:ne] = cluster_ref[...].astype(f32)
    cluster = jnp.transpose(lines_misc[0:8])[0:ne].astype(jnp.int32)
    cluster = jnp.broadcast_to(cluster[:, 0:1], (ne, LANES))
    lengths = jnp.where(cluster == 0, 4, jnp.where(cluster == 1, 2, 1))

    def fill_choices():
        source = source_ref[...]
        is_local = source < ne
        lines_misc[8:12, 0:ne] = orient_ref[...].astype(f32)
        lines_misc[16:20, 0:ne] = jnp.where(is_local, face_ref[...] * ne + source, 1000).astype(f32)
        misc = jnp.transpose(lines_misc[...])[0:ne].astype(jnp.int32)

        def column(c):
            return jnp.broadcast_to(misc[:, c : c + 1], (ne, LANES))

        turns = [
            jnp.where(left, column(8 + 2 * side), column(9 + 2 * side)) for side in range(2)
        ]
        turn_wide = jnp.concatenate(turns, axis=1)
        for i in range(4):
            hot = jnp.where(lane_mod == column(16 + i), 1.0, 0.0)
            take_loc[i * ne : (i + 1) * ne, :] = hot.astype(bf16)
        for h in range(3):
            turn_mask[h] = jnp.where(turn_wide == h, 1.0, 0.0).astype(bf16)

    for d in range(6):
        for k in range(slots):
            send_row[d * slots + k] = faces_ref[k, d] * rows + elements_ref[k, d]

    def fill_take():
        for i in range(4):
            for e in range(ne):
                place = source_scalar[i, e] - ne
                take_row[i * ne + e] = jnp.where(place < 0, 6 * slots, place)

    for q in range(nq):
        val[q * ne : (q + 1) * ne, 0:nb] = state_ref[q]

    greeted = 4 + has_prev.astype(jnp.int32) + has_next.astype(jnp.int32)

    lane4 = lax.broadcasted_iota(jnp.int32, (4, LANES), 1)

    def copy_of(s, place):
        return pltpu.make_async_remote_copy(
            src_ref=sbuf.at[s, pl.ds(place * slots, slots)],
            dst_ref=rbuf.at[s, pl.ds(place * slots, slots)],
            send_sem=send_sem.at[s, place],
            recv_sem=recv_sem.at[s, place],
            device_id=targets[place],
            device_id_type=MESH,
        )

    def apply(x_ref, table, matrices, first, total):
        for d in range(matrices):
            for q in range(nq):
                lanes = slice((first + d) * LANES, (first + d + 1) * LANES)
                term = table[q * matrices + d].reshape(nq, ne, LANES) * x_ref[q * ne : (q + 1) * ne, lanes][None]
                total = term if total is None else total + term
        return total

    def substep(s, carry):
        phase = s & (lengths - 1)
        ending = phase + 1 == lengths
        factorial = 1.0
        groups = [slice(start, start + 8) for start in range(0, ne, 8)]
        whole = val[...].reshape(nq, ne, LANES)
        derivs = [whole[:, group] for group in groups]
        for order in range(ORDER):
            factorial = factorial * (order + 1)
            coeffs = [
                np.float32((((w + 1) * 0.25) ** (order + 1) - (w * 0.25) ** (order + 1)) / factorial)
                for w in range(4)
            ]
            w_now = jnp.where(
                phase == 0,
                coeffs[0],
                jnp.where(phase == 1, coeffs[1], jnp.where(phase == 2, coeffs[2], coeffs[3])),
            )
            for group, deriv in zip(groups, derivs):
                series[order, :, group, :] = deriv
                if order == 0:
                    cur_ref[:, group, :] = w_now[group][None] * deriv
                else:
                    cur_ref[:, group, :] += w_now[group][None] * deriv
            if order + 1 < ORDER:
                for g, deriv in enumerate(derivs):
                    halfx[g] = dot(three(deriv.reshape(nq * 8, LANES)), w_ck[...])
                derivs = []
                for g, group in enumerate(groups):
                    total = None
                    for d in range(3):
                        lanes = slice(d * LANES, (d + 1) * LANES)
                        for q in range(nq):
                            table = star_table[q * 3 + d].reshape(nq, ne, LANES)[:, group]
                            term = table * halfx[g, q * 8 : (q + 1) * 8, lanes][None]
                            total = term if total is None else total + term
                    derivs.append(total)

        for g, group in enumerate(groups):
            faces = dot(three(cur_ref[:, group, :].reshape(nq * 8, LANES)), w_proj[...])
            for j in range(4):
                for q in range(nq):
                    first = j * rows + q * ne + g * 8
                    face_rows[first : first + 8] = faces[q * 8 : (q + 1) * 8, j * LANES : (j + 1) * LANES]
        @pl.when(s == 0)
        def _():
            pl.semaphore_wait(barrier, greeted)

        for place in (0, 1, 4, 5, 2, 3):
            for slot in range(place * slots, (place + 1) * slots):
                start = send_row[slot]
                parts = [face_rows[pl.ds(start + g * ne, 4, stride=3 * ne)] for g in range(3)]
                sbuf[s, slot] = jnp.where(
                    lane4 < THIRD, parts[0], jnp.where(lane4 < 2 * THIRD, parts[1], parts[2])
                )
            guarded(sends[place], lambda place=place: copy_of(s, place).start())

        @pl.when(s == 0)
        def _():
            later_weights()
            fill_flux()
            fill_choices()
            fill_take()

        side_by_side = jnp.concatenate(
            [
                jnp.concatenate(
                    [face_rows[j * rows + q * ne : j * rows + (q + 1) * ne] for j in range(4)],
                    axis=0,
                )
                for q in range(nq)
            ],
            axis=1,
        )
        stacked = jnp.concatenate(split(side_by_side), axis=0)
        near = dot(take_loc[...], stacked)
        for q in range(nq):
            where = slice(q * LANES, (q + 1) * LANES)
            for side in range(2):
                acc_ref[q, :, side * LANES : (side + 1) * LANES] += jnp.where(
                    left,
                    near[2 * side * ne : (2 * side + 1) * ne, where],
                    pltpu.roll(near[(2 * side + 1) * ne : (2 * side + 2) * ne, where], HALF, 1),
                )
        own = None
        factorial = 1.0
        for order in range(ORDER):
            factorial = factorial * (order + 1)
            w_full = jnp.where(
                cluster == 0,
                np.float32(1.0 / factorial),
                jnp.where(
                    cluster == 1,
                    np.float32(0.5 ** (order + 1) / factorial),
                    np.float32(0.25 ** (order + 1) / factorial),
                ),
            )
            term = w_full[None] * series[order]
            own = term if own is None else own + term
        xs[...] = dot(three(own.reshape(rows, LANES)), w_own[...])
        loc_ref[...] = apply(xs, local_table, 4, 3, apply(xs, star_table, 3, 0, None))

        def receive(place):
            here = slice(place * slots, (place + 1) * slots)
            copy_of(s, place).wait_recv()
            arrived[here] = rbuf[s, here]

        for place in (0, 1, 4, 5, 2, 3):
            guarded(arrives[place], lambda place=place: receive(place))
        for row in range(4 * ne):
            got_rows[pl.ds(row, 4, stride=4 * ne)] = arrived[take_row[row]]

        def got(t, i):
            return got_rows[(t * 4 + i) * ne : (t * 4 + i + 1) * ne]

        ending_wide = jnp.concatenate([ending, ending], axis=1)
        total = None
        for q in range(nq):
            t, g = divmod(q, 3)
            sides = []
            for side in range(2):
                first, second = got(t, 2 * side), got(t, 2 * side + 1)
                if g:
                    first = pltpu.roll(first, LANES - g * THIRD, 1)
                second = pltpu.roll(second, (HALF - g * THIRD) % LANES, 1)
                sides.append(jnp.where(left, first, second))
            wide = acc_ref[q] + jnp.concatenate(sides, axis=1)
            term = far_table[q].reshape(nq, ne, 2 * LANES) * wide[None]
            total = term if total is None else total + term
            acc_ref[q] = jnp.where(ending_wide, 0.0, wide)
        parts = [part.reshape(nq, ne, 2 * LANES) for part in split(total.reshape(rows, 2 * LANES))]
        high, low = [
            [(part * turn_mask[h][None]).reshape(rows, 2 * LANES) for h in range(3)] for part in parts
        ]
        masked = jnp.concatenate(
            [jnp.concatenate(high, axis=1), jnp.concatenate(low, axis=1)], axis=0
        )
        both = dot(masked, w_lift[...])
        upd = both[0:rows, 0:LANES] + both[0:rows, LANES : 2 * LANES] + both[rows:, 0:LANES]
        upd = upd.reshape(nq, ne, LANES) + loc_ref[...]
        old = val[...].reshape(nq, ne, LANES)
        val[...] = jnp.where(ending[None], old + upd, old).reshape(rows, LANES)
        return carry

    lax.fori_loop(0, SUBSTEPS, substep, 0)
    out_ref[...] = val[...].reshape(nq, ne, LANES)

    def drain(s, carry):
        for place in range(6):
            guarded(sends[place], lambda place=place: copy_of(s, place).wait_send())
        return carry

    lax.fori_loop(0, SUBSTEPS, drain, 0)


def shards(
    n_dom, n_sub,
    state, ck_matrices, vol_matrices, face_project, face_lift, face_turn,
    star_matrices, flux_local, flux_neighbor, cluster,
    send_elements, send_faces, neighbor_source, neighbor_face, neighbor_turn,
):
    nq, nb, ne = state.shape
    nf = face_project.shape[1]
    rows = nq * ne
    slots = send_elements.shape[3]
    operands = [
        state.transpose(0, 2, 1),
        ck_matrices,
        vol_matrices,
        face_project.transpose(1, 0, 2),
        face_lift.transpose(2, 0, 1),
        face_turn,
        star_matrices.transpose(1, 2, 0, 3),
        flux_local.transpose(1, 2, 0, 3),
        flux_neighbor.transpose(1, 2, 0, 3),
        cluster[None],
        send_elements[0, 0].T,
        send_faces[0, 0].T,
        neighbor_source,
        neighbor_face,
        neighbor_turn,
    ]
    whole = pl.BlockSpec(memory_space=pltpu.VMEM)
    result = pl.pallas_call(
        functools.partial(kernel, n_dom, n_sub, nq, ne, nb, nf),
        out_shape=pltpu.VMEM((nq, ne, LANES), f32),
        in_specs=[pl.BlockSpec(memory_space=pltpu.HBM)] * len(operands),
        out_specs=whole,
        scratch_shapes=[
            *[(pltpu.SMEM if k in (10, 11) else pltpu.VMEM)(x.shape, x.dtype) for k, x in enumerate(operands)],
            pltpu.SMEM(neighbor_source.shape, jnp.int32),
            pltpu.SemaphoreType.DMA((len(operands) + 1,)),
            pltpu.VMEM((30, LANES, LANES), f32),
            pltpu.VMEM((nq, 32, LANES), f32),
            pltpu.VMEM((nq, 8 * nq, LANES), f32),
            pltpu.VMEM((nq, ne, 8 * nq), f32),
            pltpu.VMEM((32, LANES), f32),
            pltpu.VMEM((3 * LANES, 3 * LANES), bf16),
            pltpu.VMEM((3 * LANES, 7 * LANES), bf16),
            pltpu.VMEM((3 * LANES, 4 * LANES), bf16),
            pltpu.VMEM((3 * 4 * HALF, 2 * LANES), bf16),
            pltpu.VMEM((2 * rows, 8 * nq), bf16),
            pltpu.VMEM((3 * nq + 1, rows, LANES), f32),
            pltpu.VMEM((4 * nq, rows, LANES), f32),
            pltpu.VMEM((nq, rows, 2 * LANES), f32),
            pltpu.VMEM((rows, LANES), f32),
            pltpu.VMEM((rows, 7 * LANES), f32),
            pltpu.VMEM((ne // 8, nq * 8, 3 * LANES), f32),
            pltpu.VMEM((ORDER, nq, ne, LANES), f32),
            pltpu.VMEM((nq, ne, LANES), f32),
            pltpu.VMEM((nq, ne, LANES), f32),
            pltpu.VMEM((nq, ne, 2 * LANES), f32),
            pltpu.VMEM((4 * ne, LANES), bf16),
            pltpu.VMEM((3, ne, 2 * LANES), bf16),
            pltpu.VMEM((4 * rows + 16 * ne, LANES), f32),
            pltpu.VMEM((4 * 4 * ne, LANES), f32),
            pltpu.SMEM((6 * slots,), jnp.int32),
            pltpu.SMEM((4 * ne,), jnp.int32),
            pltpu.VMEM((SUBSTEPS, 6 * slots, 4, LANES), f32),
            pltpu.VMEM((SUBSTEPS, 6 * slots, 4, LANES), f32),
            pltpu.VMEM((6 * slots + 1, 4, LANES), f32),
            pltpu.SemaphoreType.DMA((SUBSTEPS, 6)),
            pltpu.SemaphoreType.DMA((SUBSTEPS, 6)),
        ],
        compiler_params=pltpu.CompilerParams(
            collective_id=0, has_side_effects=True, vmem_limit_bytes=24 * 1024 * 1024
        ),
    )(*[pltpu.with_memory_space_constraint(x, pltpu.HBM) for x in operands])
    return result[:, :, 0:nb].transpose(0, 2, 1)


def solution(mesh):
    both = ("dom", "sub")
    in_specs = (
        P(None, None, both),
        P(),
        P(),
        P(),
        P(),
        P(),
        P(None, None, None, both),
        P(None, None, None, both),
        P(None, None, None, both),
        P(both),
        P("dom", "sub", None, None),
        P("dom", "sub", None, None),
        P(None, both),
        P(None, both),
        P(None, both),
    )
    return jax.shard_map(
        functools.partial(shards, mesh.shape["dom"], mesh.shape["sub"]),
        mesh=mesh,
        in_specs=in_specs,
        out_specs=P(None, None, both),
        check_vma=False,
    )
```
